32 devices in a mesh: grp: 4 (over y, x), row: 2 (over core), col: 4 (over z).
Axes of the slice: x: 2, y: 2, z: 4, core: 2. Of those that a mesh axis runs over, the one named last changes fastest.
Arguments:
- layer_windows: bfloat16 [4, 768, 16384], P(None, ('row', 'grp', 'col')), may hold values from -0.046875 to 0.046875
- sketches: bfloat16 [4, 16384, 128], P(None, 'col'), may hold values from -6 to 6
- group_of: int32 [4], replicated, may hold values from 0 to 3, each once
Outputs:
- basis: float32 [4, 768, 128], P('grp', ('row', 'col'))
- projection: float32 [4, 128, 16384], P('grp', None, 'col')
The draws below stay inside these ranges and needn't reach their ends.
Inputs may be any that keep to these rules, and one draw needn't show every extreme that they name: `group_of`: each group audits exactly one matrix.
All inputs are finite; a program needn't handle non-finite values.
Results may differ from the reference program's by a relative error of at most 0.013.
Values may be sent and summed in bfloat16 or wider, within the bound.
A program may use at most 64 MiB of HBM per device.

```python
import math
import jax
import jax.numpy as jnp
from jax import lax

COLS = 16384
RANK = 128
MATS = 4
ROWS = 768


def block_levels(stream_key, shape, split, smallest, high):
    def one(position, parts):
        heights = jax.random.uniform(jax.random.fold_in(jax.random.fold_in(stream_key, 6), position), (parts,), jnp.float32, smallest / len(split), high / len(split))
        return jnp.repeat(jnp.exp(heights), shape[position] // parts).reshape((-1,) + (1,) * (len(shape) - position - 1))

    factor_of = one(*split[0])
    for cut in split[1:]:
        factor_of = factor_of * one(*cut)
    return factor_of


def normal_values(key, dims, spread, reach, pieces=(), kind=jnp.bfloat16):
    array = spread * jax.random.normal(key, dims, jnp.float32)
    if pieces:
        array = array * block_levels(key, dims, pieces, -0.22, 0.18)
    return jnp.clip(array, -reach, reach).astype(kind)


def setup_inputs(seed: int = 0) -> dict:
    arg_keys = jax.random.split(jax.random.key(seed), 4)
    layer_windows = normal_values(arg_keys[0], (MATS, ROWS, COLS), COLS ** -0.5, 0.046875, ((1, 32),))
    sketches = normal_values(arg_keys[1], (MATS, COLS, RANK), 1.0, 6.0, ((1, 4),))
    group_of = jax.random.permutation(arg_keys[2], MATS).astype(jnp.int32)
    return dict(layer_windows=layer_windows, sketches=sketches, group_of=group_of)


def right_solve(lower, power):
    return lax.linalg.triangular_solve(lower, power, left_side=False, lower=True, transpose_a=True)

def reference(layer_windows, sketches, group_of):
    slots = jnp.arange(MATS, dtype=jnp.int32)
    matched = (group_of[None, :] == slots[:, None]).astype(jnp.int32)
    owner_of = lax.optimization_barrier(jnp.sum(matched * slots[None, :], axis=1)).astype(jnp.int32)
    bases = []
    projections = []
    for slot in range(MATS):
        mine = owner_of[slot]
        matrix = lax.dynamic_index_in_dim(layer_windows, mine, 0, keepdims=False)
        omega = lax.dynamic_index_in_dim(sketches, mine, 0, keepdims=False)
        sketched = jnp.dot(matrix.astype(jnp.float32), omega.astype(jnp.float32), preferred_element_type=jnp.float32).astype(jnp.bfloat16)
        back = jnp.dot(matrix.T.astype(jnp.float32), sketched.astype(jnp.float32), preferred_element_type=jnp.float32).astype(jnp.bfloat16)
        power = jnp.dot(matrix.astype(jnp.float32), back.astype(jnp.float32), preferred_element_type=jnp.float32)
        gram = jnp.dot(power.T, power, precision=lax.Precision.HIGHEST)
        lower = jnp.linalg.cholesky(gram)
        ortho = right_solve(lower, power) * math.sqrt(ROWS)
        ortho_low = ortho.astype(jnp.bfloat16)
        proj = jnp.dot(ortho_low.T.astype(jnp.float32), matrix.astype(jnp.float32), preferred_element_type=jnp.float32) * math.sqrt(COLS / ROWS)
        bases.append(ortho)
        projections.append(proj)
    return (jnp.stack(bases), jnp.stack(projections))
```

```python
import functools
import math

import jax
import jax.numpy as jnp
from jax import lax
from jax.experimental import pallas as pl
from jax.experimental.pallas import tpu as pltpu
from jax.sharding import PartitionSpec as P

MESH = pl.DeviceIdType.MESH
F32 = jnp.float32
BF16 = jnp.bfloat16


def across(left, right):
    return lax.dot_general(
        left, right, (((0,), (0,)), ((), ())), preferred_element_type=jnp.float32
    )


def right_solve(lower, power):
    return lax.linalg.triangular_solve(lower, power, left_side=False, lower=True, transpose_a=True)


def owners(group_of):
    count = group_of.shape[0]
    slots = jnp.arange(count, dtype=jnp.int32)
    matched = (group_of[None, :] == slots[:, None]).astype(jnp.int32)
    return jnp.sum(matched * slots[None, :], axis=1)


def per_device(layer_windows, sketches, group_of):
    owner_of = owners(group_of)
    ordered = jnp.stack([
        lax.dynamic_index_in_dim(layer_windows, owner_of[j], 0, keepdims=False)
        for j in range(layer_windows.shape[0])
    ])
    block = lax.all_to_all(
        lax.all_to_all(ordered, "col", split_axis=2, concat_axis=1, tiled=True),
        "grp",
        split_axis=0,
        concat_axis=1,
        tiled=True,
    )[0]
    mine = owner_of[lax.axis_index("grp")]
    omega = lax.dynamic_index_in_dim(sketches, mine, 0, keepdims=False)
    total_rows = block.shape[0] * lax.axis_size("row")
    total_cols = block.shape[1] * lax.axis_size("col")
    share = block.shape[0] // lax.axis_size("col")

    def summed_rows(right):
        return lax.psum(jnp.dot(block, right, preferred_element_type=jnp.float32), "col")

    sketched = summed_rows(omega).astype(jnp.bfloat16)
    back = lax.psum(across(block, sketched).astype(jnp.bfloat16), "row")
    power = summed_rows(back)
    gram = lax.psum(
        jnp.dot(power.T, power, precision=lax.Precision.HIGHEST).astype(jnp.bfloat16), "row"
    ).astype(jnp.float32)
    lower = jnp.linalg.cholesky(gram)
    ortho = right_solve(lower, power) * math.sqrt(total_rows)
    basis_share = lax.dynamic_slice_in_dim(ortho, lax.axis_index("col") * share, share, 0)
    ortho_low = ortho.astype(jnp.bfloat16)
    projected = lax.psum(across(ortho_low, block).astype(jnp.bfloat16), "row").astype(
        jnp.float32
    ) * math.sqrt(total_cols / total_rows)
    return (basis_share[None], projected[None])


def inverse_factor(gram, size):
    rank = gram.shape[0]
    line = lax.broadcasted_iota(jnp.int32, (size, rank), 0)
    down = lax.broadcasted_iota(jnp.int32, (rank, rank), 0)
    eye = (down == lax.broadcasted_iota(jnp.int32, (rank, rank), 1)).astype(F32)
    rest = jnp.concatenate([gram, eye], axis=1)
    done = []
    for p in range(0, rank, size):
        top, rest = rest[:size], rest[size:]
        left, right = top[:, :rank], top[:, rank:]
        cols = [jnp.broadcast_to(left[:, p + k:p + k + 1], (size, rank)) for k in range(size)]
        pivots = jnp.zeros((size, rank), F32)
        for k in range(size):
            pivot = cols[k][k:k + 1, :]
            pivots = jnp.where(line == k, pivot, pivots)
            if k == size - 1:
                break
            factor = jnp.where(line > k, cols[k] * (1.0 / pivot), 0.0)
            for l in range(k + 1, size):
                cols[l] = cols[l] - factor * cols[l][k:k + 1, :]
            left = left - factor * left[k:k + 1, :]
            right = right - factor * right[k:k + 1, :]
        done.append(right * lax.rsqrt(pivots))
        if p + size < rank:
            weights = left * (1.0 / pivots)
            rest = rest - lax.dot_general(
                weights[:, p + size:], jnp.concatenate([left, right], axis=1),
                (((0,), (0,)), ((), ())), precision=lax.Precision.HIGHEST,
                preferred_element_type=F32)
    return jnp.concatenate(done, axis=0)


def partner(index, step):
    return (index, index + 1 - 2 * lax.rem(index, 2), lax.rem(index + 2, 4), 3 - index)[step]


HOPS = (3, 2, 1)
NT = (((1,), (1,)), ((), ()))


def range_kernel(cuts, group_of, windows, sketches, basis, projection,
                 held0, held1, held2, held3, stage, taken, pieces, block, kernel_rows, part1, part2, rs1, rs2, sk, power,
                 shown, in_sem, om_sem, out_sem, a_send, a_recv, f_send, f_recv,
                 s1_send, s1_recv, g1_send, g1_recv, h1_send, h1_recv,
                 s2_send, s2_recv, g2_send, g2_recv, h2_send, h2_recv):
    g, r, c = lax.axis_index("grp"), lax.axis_index("row"), lax.axis_index("col")
    height = windows.shape[1]
    rows, wide = block.shape
    deep, share = rows // 2, rows // 8
    root = math.sqrt(rows)
    other = (g, 1 - r, c)

    def columns(z):
        return pl.ds(pl.multiple_of(z * wide, 128), wide)

    held = (held0, held1, held2, held3)
    loads = {}
    for dz in HOPS + (0,):
        loads[dz] = pltpu.make_async_copy(
            windows.at[:, :, columns(partner(c, dz))], held[dz], in_sem.at[dz])
        loads[dz].start()
    load_omega = pltpu.make_async_copy(sketches, taken, om_sem)
    load_omega.start()

    barrier = pltpu.get_barrier_semaphore()
    for dz in range(4):
        for dg in range(4):
            if dz or dg:
                pl.semaphore_signal(barrier, inc=1, device_id=(partner(g, dg), r, partner(c, dz)),
                                    device_id_type=MESH)
    pl.semaphore_signal(barrier, inc=1, device_id=other, device_id_type=MESH)

    def owner(slot):
        found = jnp.int32(0)
        for m in range(4):
            found = jnp.where(group_of[m] == slot, jnp.int32(m), found)
        return found

    sources = [owner(partner(g, dg)) for dg in range(4)]
    across_order = [(dz, dg) for dg in (3, 1, 2, 0) for dz in (2, 3)]
    near_order = [(dz, dg) for dz in (0, 1) for dg in (3, 1, 2, 0)]

    sends = {}

    def send(dz, dg):
        copy = pltpu.make_async_remote_copy(
            src_ref=stage.at[dz, dg], dst_ref=pieces.at[r, g, c],
            send_sem=a_send.at[dz, dg], recv_sem=a_recv.at[dz, dg],
            device_id=(partner(g, dg), r, partner(c, dz)), device_id_type=MESH)
        copy.start()
        sends[dz, dg] = copy

    for dz in (2, 3, 0, 1):
        loads[dz].wait()
        for dg in range(4):
            if dz or dg:
                stage[dz, dg] = held[dz][sources[dg]]
            else:
                pieces[r, g, c] = held[0][sources[0]]
        if dz == 3:
            pl.semaphore_wait(barrier, 16)
            for dz_, dg in across_order:
                send(dz_, dg)
    for dz, dg in near_order:
        if dz or dg:
            send(dz, dg)
    load_omega.wait()
    omega = taken[sources[0]]

    forwards = {}

    def forward(dz, dg):
        spot = pieces.at[r, partner(g, dg), partner(c, dz)]
        copy = pltpu.make_async_remote_copy(
            src_ref=spot, dst_ref=spot, send_sem=f_send.at[dz, dg], recv_sem=f_recv.at[dz, dg],
            device_id=other, device_id_type=MESH)
        copy.start()
        forwards[dz, dg] = copy

    def pair_rows(side, dg, far):
        half = lax.rem(c // 2 + far, 2)
        start = ((side * 4 + partner(g, dg)) * 4 + 2 * half) * height
        return half, pl.ds(pl.multiple_of(start, 16), 2 * height)

    def settle(side, dg, far):
        half, place = pair_rows(side, dg, far)
        block[place, :] = pieces[side, partner(g, dg), pl.ds(2 * half, 2)].reshape(2 * height, wide)
        return half, place

    def sketch(dg, far):
        half, place = settle(r, dg, far)
        done = jnp.dot(block[place, :], omega, preferred_element_type=F32)
        into = pl.ds(pl.multiple_of(2 * height * half, 16), 2 * height)
        part1[partner(g, dg), into, :] = done.astype(BF16)

    pairs = [(dg, 0) for dg in (3, 1, 2, 0)] + [(dg, 1) for dg in (3, 1, 2, 0)]
    for i, (dg, far) in enumerate(pairs):
        for dz in ((0, 1), (2, 3))[far]:
            if dz or dg:
                sends[dz, dg].wait_recv()
            forward(dz, dg)
        if i:
            before = pairs[i - 1]
            for dz in ((0, 1), (2, 3))[before[1]]:
                forwards[dz, before[0]].wait_recv()
            settle(1 - r, *before)
        sketch(dg, far)

    def scatter(part, rs, send_sem, recv_sem):
        copies = []
        for dz in HOPS:
            k = partner(c, dz)
            copy = pltpu.make_async_remote_copy(
                src_ref=part.at[k], dst_ref=rs.at[dz], send_sem=send_sem.at[dz],
                recv_sem=recv_sem.at[dz], device_id=(g, r, k), device_id_type=MESH)
            copy.start()
            copies.append(copy)
        return copies

    def total(part, rs, copies):
        for copy in copies:
            copy.wait()
        found = part[c].astype(F32)
        for dz in HOPS:
            found = found + rs[dz].astype(F32)
        return found

    def gather(ref, g_send, g_recv, h_send, h_recv):
        def spot(k):
            return ref.at[pl.ds(pl.multiple_of(r * deep + k * share, 16), share), :]

        copies, passed = [], []

        def hand(dz):
            place = spot(partner(c, dz))
            copy = pltpu.make_async_remote_copy(
                src_ref=place, dst_ref=place, send_sem=h_send.at[dz], recv_sem=h_recv.at[dz],
                device_id=other, device_id_type=MESH)
            copy.start()
            passed.append(copy)

        for dz in HOPS:
            copy = pltpu.make_async_remote_copy(
                src_ref=spot(c), dst_ref=spot(c), send_sem=g_send.at[dz], recv_sem=g_recv.at[dz],
                device_id=(g, r, partner(c, dz)), device_id_type=MESH)
            copy.start()
            copies.append((dz, copy))
        hand(0)
        for dz, copy in reversed(copies):
            copy.wait_recv()
            hand(dz)

        def finish():
            for _, copy in copies:
                copy.wait_send()
            for copy in passed:
                copy.wait()
        return finish

    def own_rows(side):
        return pl.ds(pl.multiple_of(side * deep, 16), deep)

    copies = scatter(part1, rs1, s1_send, s1_recv)
    last = pairs[-1]
    for dz in (2, 3):
        forwards[dz, last[0]].wait_recv()
    settle(1 - r, *last)
    found = lax.dot_general(block[own_rows(r), :], block[...], NT, preferred_element_type=F32)
    kernel_rows[...] = found.astype(BF16)
    sk[pl.ds(pl.multiple_of(r * deep + c * share, 16), share), :] = total(
        part1, rs1, copies).astype(BF16)
    gather(sk, g1_send, g1_recv, h1_send, h1_recv)()

    found = jnp.dot(kernel_rows[...], sk[...], preferred_element_type=F32)
    for k in range(4):
        part2[k] = found[k * share:(k + 1) * share, :].astype(BF16)
    mine = total(part2, rs2, scatter(part2, rs2, s2_send, s2_recv))
    power[pl.ds(pl.multiple_of(r * deep + c * share, 16), share), :] = mine.astype(BF16)
    gather(power, g2_send, g2_recv, h2_send, h2_recv)()

    whole = power[...]
    gram = lax.dot_general(whole, whole, (((0,), (0,)), ((), ())), preferred_element_type=F32)
    inverse = inverse_factor(gram, 32)
    turned = (lax.dot_general(inverse, whole.astype(F32), NT, precision=lax.Precision.HIGHEST,
                              preferred_element_type=F32) * root).astype(BF16)
    step = wide // cuts
    scale = math.sqrt(4 * wide / rows)
    outs = []
    for i in range(cuts):
        span = pl.ds(i * step, step)
        shown[:, span] = jnp.dot(turned, block[:, span], preferred_element_type=F32) * scale
        copy = pltpu.make_async_copy(shown.at[:, span], projection.at[:, span], out_sem.at[i])
        copy.start()
        outs.append(copy)
    basis[...] = lax.dot_general(mine, inverse, NT, precision=lax.Precision.HIGHEST,
                                 preferred_element_type=F32) * root
    for copy in sends.values():
        copy.wait_send()
    for copy in forwards.values():
        copy.wait_send()
    for copy in outs:
        copy.wait()


def fused_device(layer_windows, sketches, group_of):
    _, height, total_cols = layer_windows.shape
    rank = sketches.shape[2]
    wide = total_cols // 4
    rows = height * 32
    share = rows // 8
    cuts = 8
    anywhere = pl.BlockSpec(memory_space=pl.ANY)
    dma = pltpu.SemaphoreType.DMA
    basis, projection = pl.pallas_call(
        functools.partial(range_kernel, cuts),
        out_shape=(
            jax.ShapeDtypeStruct((share, rank), F32),
            jax.ShapeDtypeStruct((rank, wide), F32),
        ),
        in_specs=[pl.BlockSpec(memory_space=pltpu.SMEM), anywhere, anywhere],
        out_specs=(pl.BlockSpec(memory_space=pltpu.VMEM), anywhere),
        scratch_shapes=[
            *[pltpu.VMEM((4, height, wide), BF16)] * 4,
            pltpu.VMEM((4, 4, height, wide), BF16),
            pltpu.VMEM(sketches.shape, BF16),
            pltpu.VMEM((2, 4, 4, height, wide), BF16),
            pltpu.VMEM((rows, wide), BF16),
            pltpu.VMEM((rows // 2, rows), BF16),
            pltpu.VMEM((4, share, rank), BF16),
            pltpu.VMEM((4, share, rank), BF16),
            pltpu.VMEM((4, share, rank), BF16),
            pltpu.VMEM((4, share, rank), BF16),
            pltpu.VMEM((rows, rank), BF16),
            pltpu.VMEM((rows, rank), BF16),
            pltpu.VMEM((rank, wide), F32),
            dma((4,)), dma, dma((cuts,)),
            dma((4, 4)), dma((4, 4)), dma((4, 4)), dma((4, 4)),
            dma((4,)), dma((4,)), dma((4,)), dma((4,)), dma((4,)), dma((4,)),
            dma((4,)), dma((4,)), dma((4,)), dma((4,)), dma((4,)), dma((4,)),
        ],
        compiler_params=pltpu.CompilerParams(
            collective_id=0, has_side_effects=True, vmem_limit_bytes=56 << 20),
        name="range_finder",
    )(group_of, layer_windows, sketches)
    return basis[None], projection[None]


def solution(mesh):
    in_specs = (P(None, ("row", "grp", "col"), None), P(None, "col", None), P())
    out_specs = (P("grp", ("row", "col"), None), P("grp", None, "col"))
    sizes = (mesh.shape["grp"], mesh.shape["row"], mesh.shape["col"])

    def body(layer_windows, sketches, group_of):
        count, height, total_cols = layer_windows.shape
        fits = sizes == (4, 2, 4) and count == 4 and height % 8 == 0 and height <= 32
        if fits and sketches.shape[2] == 128 and total_cols in (8192, 16384):
            return fused_device(layer_windows, sketches, group_of)
        return per_device(layer_windows, sketches, group_of)

    return jax.shard_map(body, mesh=mesh, in_specs=in_specs, out_specs=out_specs, check_vma=False)
```

```python
import functools
import math

import jax
import jax.numpy as jnp
from jax import lax
from jax.experimental import pallas as pl
from jax.experimental.pallas import tpu as pltpu
from jax.sharding import PartitionSpec as P

MESH = pl.DeviceIdType.MESH
F32 = jnp.float32
BF16 = jnp.bfloat16


def across(left, right):
    return lax.dot_general(
        left, right, (((0,), (0,)), ((), ())), preferred_element_type=jnp.float32
    )


def right_solve(lower, power):
    return lax.linalg.triangular_solve(lower, power, left_side=False, lower=True, transpose_a=True)


def owners(group_of):
    count = group_of.shape[0]
    slots = jnp.arange(count, dtype=jnp.int32)
    matched = (group_of[None, :] == slots[:, None]).astype(jnp.int32)
    return jnp.sum(matched * slots[None, :], axis=1)


def per_device(layer_windows, sketches, group_of):
    owner_of = owners(group_of)
    ordered = jnp.stack([
        lax.dynamic_index_in_dim(layer_windows, owner_of[j], 0, keepdims=False)
        for j in range(layer_windows.shape[0])
    ])
    block = lax.all_to_all(
        lax.all_to_all(ordered, "col", split_axis=2, concat_axis=1, tiled=True),
        "grp",
        split_axis=0,
        concat_axis=1,
        tiled=True,
    )[0]
    mine = owner_of[lax.axis_index("grp")]
    omega = lax.dynamic_index_in_dim(sketches, mine, 0, keepdims=False)
    total_rows = block.shape[0] * lax.axis_size("row")
    total_cols = block.shape[1] * lax.axis_size("col")
    share = block.shape[0] // lax.axis_size("col")

    def summed_rows(right):
        return lax.psum(jnp.dot(block, right, preferred_element_type=jnp.float32), "col")

    sketched = summed_rows(omega).astype(jnp.bfloat16)
    back = lax.psum(across(block, sketched).astype(jnp.bfloat16), "row")
    power = summed_rows(back)
    gram = lax.psum(
        jnp.dot(power.T, power, precision=lax.Precision.HIGHEST).astype(jnp.bfloat16), "row"
    ).astype(jnp.float32)
    lower = jnp.linalg.cholesky(gram)
    ortho = right_solve(lower, power) * math.sqrt(total_rows)
    basis_share = lax.dynamic_slice_in_dim(ortho, lax.axis_index("col") * share, share, 0)
    ortho_low = ortho.astype(jnp.bfloat16)
    projected = lax.psum(across(ortho_low, block).astype(jnp.bfloat16), "row").astype(
        jnp.float32
    ) * math.sqrt(total_cols / total_rows)
    return (basis_share[None], projected[None])


def inverse_factor(gram, size):
    rank = gram.shape[0]
    line = lax.broadcasted_iota(jnp.int32, (size, rank), 0)
    down = lax.broadcasted_iota(jnp.int32, (rank, rank), 0)
    eye = (down == lax.broadcasted_iota(jnp.int32, (rank, rank), 1)).astype(F32)
    rest = jnp.concatenate([gram, eye], axis=1)
    done = []
    for p in range(0, rank, size):
        top, rest = rest[:size], rest[size:]
        left, right = top[:, :rank], top[:, rank:]
        cols = [jnp.broadcast_to(left[:, p + k:p + k + 1], (size, rank)) for k in range(size)]
        pivots = jnp.zeros((size, rank), F32)
        for k in range(size):
            pivot = cols[k][k:k + 1, :]
            pivots = jnp.where(line == k, pivot, pivots)
            if k == size - 1:
                break
            factor = jnp.where(line > k, cols[k] * (1.0 / pivot), 0.0)
            for l in range(k + 1, size):
                cols[l] = cols[l] - factor * cols[l][k:k + 1, :]
            left = left - factor * left[k:k + 1, :]
            right = right - factor * right[k:k + 1, :]
        done.append(right * lax.rsqrt(pivots))
        if p + size < rank:
            weights = left * (1.0 / pivots)
            rest = rest - lax.dot_general(
                weights[:, p + size:], jnp.concatenate([left, right], axis=1),
                (((0,), (0,)), ((), ())), precision=lax.Precision.HIGHEST,
                preferred_element_type=F32)
    return jnp.concatenate(done, axis=0)


def partner(index, step):
    return (index, index + 1 - 2 * lax.rem(index, 2), lax.rem(index + 2, 4), 3 - index)[step]


HOPS = (3, 2, 1)
NT = (((1,), (1,)), ((), ()))


def range_kernel(cuts, group_of, windows, sketches, basis, projection,
                 held0, held1, held2, held3, stage, taken, pieces, block, kernel_rows, part1, part2, rs1, rs2, sk, power,
                 in_sem, om_sem, a_send, a_recv, f_send, f_recv,
                 s1_send, s1_recv, g1_send, g1_recv, h1_send, h1_recv,
                 s2_send, s2_recv, g2_send, g2_recv, h2_send, h2_recv):
    g, r, c = lax.axis_index("grp"), lax.axis_index("row"), lax.axis_index("col")
    height = windows.shape[1]
    rows, wide = block.shape
    deep, share = rows // 2, rows // 8
    root = math.sqrt(rows)
    other = (g, 1 - r, c)

    def columns(z):
        return pl.ds(pl.multiple_of(z * wide, 128), wide)

    held = (held0, held1, held2, held3)
    loads = {}
    for dz in (2, 3, 1, 0):
        loads[dz] = pltpu.make_async_copy(
            windows.at[:, :, columns(partner(c, dz))], held[dz], in_sem.at[dz])
        loads[dz].start()
    barrier = pltpu.get_barrier_semaphore()
    for dz in range(4):
        for dg in range(4):
            if dz or dg:
                pl.semaphore_signal(barrier, inc=1, device_id=(partner(g, dg), r, partner(c, dz)),
                                    device_id_type=MESH)
    pl.semaphore_signal(barrier, inc=1, device_id=other, device_id_type=MESH)

    def owner(slot):
        found = jnp.int32(0)
        for m in range(4):
            found = jnp.where(group_of[m] == slot, jnp.int32(m), found)
        return found

    sources = [owner(partner(g, dg)) for dg in range(4)]
    across_order = [(dz, dg) for dg in range(4) for dz in (2, 3)]
    near_order = [(dz, dg) for dz in (1, 0) for dg in (3, 1, 2, 0)]

    sends = {}

    def send(dz, dg):
        copy = pltpu.make_async_remote_copy(
            src_ref=stage.at[dz, dg], dst_ref=pieces.at[r, g, c],
            send_sem=a_send.at[dz, dg], recv_sem=a_recv.at[dz, dg],
            device_id=(partner(g, dg), r, partner(c, dz)), device_id_type=MESH)
        copy.start()
        sends[dz, dg] = copy

    for dz in (2, 3, 1, 0):
        loads[dz].wait()
        for dg in range(4):
            if dz or dg:
                stage[dz, dg] = held[dz][sources[dg]]
            else:
                pieces[r, g, c] = held[0][sources[0]]
        if dz == 3:
            pl.semaphore_wait(barrier, 16)
            for dz_, dg in across_order:
                send(dz_, dg)
    for dz, dg in near_order:
        if dz or dg:
            send(dz, dg)
    load_omega = pltpu.make_async_copy(sketches, taken, om_sem)
    load_omega.start()
    load_omega.wait()
    omega = taken[sources[0]]

    forwards = {}

    def forward(dz, dg):
        spot = pieces.at[r, partner(g, dg), partner(c, dz)]
        copy = pltpu.make_async_remote_copy(
            src_ref=spot, dst_ref=spot, send_sem=f_send.at[dz, dg], recv_sem=f_recv.at[dz, dg],
            device_id=other, device_id_type=MESH)
        copy.start()
        forwards[dz, dg] = copy

    def pair_rows(side, dg, far):
        half = lax.rem(c // 2 + far, 2)
        start = ((side * 4 + partner(g, dg)) * 4 + 2 * half) * height
        return half, pl.ds(pl.multiple_of(start, 16), 2 * height)

    def settle(side, dg, far):
        half, place = pair_rows(side, dg, far)
        block[place, :] = pieces[side, partner(g, dg), pl.ds(2 * half, 2)].reshape(2 * height, wide)
        return half, place

    def sketch(dg, far):
        half, place = settle(r, dg, far)
        done = jnp.dot(block[place, :], omega, preferred_element_type=F32)
        into = pl.ds(pl.multiple_of(2 * height * half, 16), 2 * height)
        part1[partner(g, dg), into, :] = done.astype(BF16)

    pairs = [(dg, 0) for dg in (3, 1, 2, 0)] + [(dg, 1) for dg in range(4)]
    for i, (dg, far) in enumerate(pairs):
        for dz in ((0, 1), (2, 3))[far]:
            if dz or dg:
                sends[dz, dg].wait_recv()
            forward(dz, dg)
        if i:
            before = pairs[i - 1]
            for dz in ((0, 1), (2, 3))[before[1]]:
                forwards[dz, before[0]].wait_recv()
            settle(1 - r, *before)
        sketch(dg, far)

    def scatter(part, rs, send_sem, recv_sem):
        copies = []
        for dz in HOPS:
            k = partner(c, dz)
            copy = pltpu.make_async_remote_copy(
                src_ref=part.at[k], dst_ref=rs.at[dz], send_sem=send_sem.at[dz],
                recv_sem=recv_sem.at[dz], device_id=(g, r, k), device_id_type=MESH)
            copy.start()
            copies.append(copy)
        return copies

    def total(part, rs, copies):
        for copy in copies:
            copy.wait()
        found = part[c].astype(F32)
        for dz in HOPS:
            found = found + rs[dz].astype(F32)
        return found

    def gather(ref, g_send, g_recv, h_send, h_recv):
        def spot(k):
            return ref.at[pl.ds(pl.multiple_of(r * deep + k * share, 16), share), :]

        copies, passed = [], []

        def hand(dz):
            place = spot(partner(c, dz))
            copy = pltpu.make_async_remote_copy(
                src_ref=place, dst_ref=place, send_sem=h_send.at[dz], recv_sem=h_recv.at[dz],
                device_id=other, device_id_type=MESH)
            copy.start()
            passed.append(copy)

        for dz in HOPS:
            copy = pltpu.make_async_remote_copy(
                src_ref=spot(c), dst_ref=spot(c), send_sem=g_send.at[dz], recv_sem=g_recv.at[dz],
                device_id=(g, r, partner(c, dz)), device_id_type=MESH)
            copy.start()
            copies.append((dz, copy))
        hand(0)
        for dz, copy in reversed(copies):
            copy.wait_recv()
            hand(dz)

        def finish():
            for _, copy in copies:
                copy.wait_send()
            for copy in passed:
                copy.wait()
        return finish

    def own_rows(side):
        return pl.ds(pl.multiple_of(side * deep, 16), deep)

    copies = scatter(part1, rs1, s1_send, s1_recv)
    last = pairs[-1]
    for dz in (2, 3):
        forwards[dz, last[0]].wait_recv()
    settle(1 - r, *last)
    found = lax.dot_general(block[own_rows(r), :], block[...], NT, preferred_element_type=F32)
    kernel_rows[...] = found.astype(BF16)
    sk[pl.ds(pl.multiple_of(r * deep + c * share, 16), share), :] = total(
        part1, rs1, copies).astype(BF16)
    gather(sk, g1_send, g1_recv, h1_send, h1_recv)()

    found = jnp.dot(kernel_rows[...], sk[...], preferred_element_type=F32)
    for k in range(4):
        part2[k] = found[k * share:(k + 1) * share, :].astype(BF16)
    mine = total(part2, rs2, scatter(part2, rs2, s2_send, s2_recv))
    power[pl.ds(pl.multiple_of(r * deep + c * share, 16), share), :] = mine.astype(BF16)
    gather(power, g2_send, g2_recv, h2_send, h2_recv)()

    whole = power[...]
    gram = lax.dot_general(whole, whole, (((0,), (0,)), ((), ())), preferred_element_type=F32)
    inverse = inverse_factor(gram, 32)
    turned = (lax.dot_general(inverse, whole.astype(F32), NT, precision=lax.Precision.HIGHEST,
                              preferred_element_type=F32) * root).astype(BF16)
    step = wide // cuts
    scale = math.sqrt(4 * wide / rows)
    for i in range(cuts):
        span = pl.ds(i * step, step)
        projection[:, span] = jnp.dot(turned, block[:, span], preferred_element_type=F32) * scale
    basis[...] = lax.dot_general(mine, inverse, NT, precision=lax.Precision.HIGHEST,
                                 preferred_element_type=F32) * root
    for copy in sends.values():
        copy.wait_send()
    for copy in forwards.values():
        copy.wait_send()


def write_kernel(basis, projection, basis_out, projection_out, basis_sem, projection_sem):
    first = pltpu.make_async_copy(projection, projection_out.at[0], projection_sem)
    first.start()
    second = pltpu.make_async_copy(basis, basis_out.at[0], basis_sem)
    second.start()
    first.wait()
    second.wait()


def fused_device(layer_windows, sketches, group_of):
    _, height, total_cols = layer_windows.shape
    rank = sketches.shape[2]
    wide = total_cols // 4
    rows = height * 32
    share = rows // 8
    cuts = 8
    vmem = pl.BlockSpec(memory_space=pltpu.VMEM)
    hbm = pl.BlockSpec(memory_space=pltpu.HBM)
    dma = pltpu.SemaphoreType.DMA
    basis, projection = pl.pallas_call(
        functools.partial(range_kernel, cuts),
        out_shape=(
            jax.ShapeDtypeStruct((share, rank), F32),
            jax.ShapeDtypeStruct((rank, wide), F32),
        ),
        in_specs=[pl.BlockSpec(memory_space=pltpu.SMEM), hbm, hbm],
        out_specs=(vmem, vmem),
        scratch_shapes=[
            *[pltpu.VMEM((4, height, wide), BF16)] * 4,
            pltpu.VMEM((4, 4, height, wide), BF16),
            pltpu.VMEM(sketches.shape, BF16),
            pltpu.VMEM((2, 4, 4, height, wide), BF16),
            pltpu.VMEM((rows, wide), BF16),
            pltpu.VMEM((rows // 2, rows), BF16),
            pltpu.VMEM((4, share, rank), BF16),
            pltpu.VMEM((4, share, rank), BF16),
            pltpu.VMEM((4, share, rank), BF16),
            pltpu.VMEM((4, share, rank), BF16),
            pltpu.VMEM((rows, rank), BF16),
            pltpu.VMEM((rows, rank), BF16),
            dma((4,)), dma,
            dma((4, 4)), dma((4, 4)), dma((4, 4)), dma((4, 4)),
            dma((4,)), dma((4,)), dma((4,)), dma((4,)), dma((4,)), dma((4,)),
            dma((4,)), dma((4,)), dma((4,)), dma((4,)), dma((4,)), dma((4,)),
        ],
        compiler_params=pltpu.CompilerParams(
            collective_id=0, has_side_effects=True, vmem_limit_bytes=50 << 20),
        name="range_finder",
    )(group_of, layer_windows, sketches)
    return pl.pallas_call(
        write_kernel,
        out_shape=(
            jax.ShapeDtypeStruct((1, share, rank), F32),
            jax.ShapeDtypeStruct((1, rank, wide), F32),
        ),
        in_specs=[vmem, vmem],
        out_specs=(hbm, hbm),
        scratch_shapes=[dma, dma],
        compiler_params=pltpu.CompilerParams(vmem_limit_bytes=8 << 20),
        name="write_out",
    )(basis, projection)


def solution(mesh):
    in_specs = (P(None, ("row", "grp", "col"), None), P(None, "col", None), P())
    out_specs = (P("grp", ("row", "col"), None), P("grp", None, "col"))
    sizes = (mesh.shape["grp"], mesh.shape["row"], mesh.shape["col"])

    def body(layer_windows, sketches, group_of):
        count, height, total_cols = layer_windows.shape
        fits = sizes == (4, 2, 4) and count == 4 and height % 8 == 0 and height <= 32
        if fits and sketches.shape[2] == 128 and total_cols in (8192, 16384):
            return fused_device(layer_windows, sketches, group_of)
        return per_device(layer_windows, sketches, group_of)

    return jax.shard_map(body, mesh=mesh, in_specs=in_specs, out_specs=out_specs, check_vma=False)
```

```python
import functools
import math

import jax
import jax.numpy as jnp
from jax import lax
from jax.experimental import pallas as pl
from jax.experimental.pallas import tpu as pltpu
from jax.sharding import PartitionSpec as P

MESH = pl.DeviceIdType.MESH
F32 = jnp.float32
BF16 = jnp.bfloat16


def across(left, right):
    return lax.dot_general(
        left, right, (((0,), (0,)), ((), ())), preferred_element_type=jnp.float32
    )


def right_solve(lower, power):
    return lax.linalg.triangular_solve(lower, power, left_side=False, lower=True, transpose_a=True)


def owners(group_of):
    count = group_of.shape[0]
    slots = jnp.arange(count, dtype=jnp.int32)
    matched = (group_of[None, :] == slots[:, None]).astype(jnp.int32)
    return jnp.sum(matched * slots[None, :], axis=1)


def per_device(layer_windows, sketches, group_of):
    owner_of = owners(group_of)
    ordered = jnp.stack([
        lax.dynamic_index_in_dim(layer_windows, owner_of[j], 0, keepdims=False)
        for j in range(layer_windows.shape[0])
    ])
    block = lax.all_to_all(
        lax.all_to_all(ordered, "col", split_axis=2, concat_axis=1, tiled=True),
        "grp",
        split_axis=0,
        concat_axis=1,
        tiled=True,
    )[0]
    mine = owner_of[lax.axis_index("grp")]
    omega = lax.dynamic_index_in_dim(sketches, mine, 0, keepdims=False)
    total_rows = block.shape[0] * lax.axis_size("row")
    total_cols = block.shape[1] * lax.axis_size("col")
    share = block.shape[0] // lax.axis_size("col")

    def summed_rows(right):
        return lax.psum(jnp.dot(block, right, preferred_element_type=jnp.float32), "col")

    sketched = summed_rows(omega).astype(jnp.bfloat16)
    back = lax.psum(across(block, sketched).astype(jnp.bfloat16), "row")
    power = summed_rows(back)
    gram = lax.psum(
        jnp.dot(power.T, power, precision=lax.Precision.HIGHEST).astype(jnp.bfloat16), "row"
    ).astype(jnp.float32)
    lower = jnp.linalg.cholesky(gram)
    ortho = right_solve(lower, power) * math.sqrt(total_rows)
    basis_share = lax.dynamic_slice_in_dim(ortho, lax.axis_index("col") * share, share, 0)
    ortho_low = ortho.astype(jnp.bfloat16)
    projected = lax.psum(across(ortho_low, block).astype(jnp.bfloat16), "row").astype(
        jnp.float32
    ) * math.sqrt(total_cols / total_rows)
    return (basis_share[None], projected[None])


def thirds(array):
    high = array.astype(BF16)
    rest = array - high.astype(F32)
    middle = rest.astype(BF16)
    return high, middle, (rest - middle.astype(F32)).astype(BF16)


def across_rows(left, right):
    a, b, c = thirds(left)
    d, e, f = thirds(right)
    return lax.dot_general(
        jnp.concatenate([a, a, b, a, b, c], axis=0), jnp.concatenate([d, e, d, f, e, d], axis=0),
        (((0,), (0,)), ((), ())), preferred_element_type=F32)


def inverse_factor(gram, size):
    rank = gram.shape[0]
    tiles = size // 8
    line = lax.broadcasted_iota(jnp.int32, (8, rank), 0)
    down = lax.broadcasted_iota(jnp.int32, (rank, rank), 0)
    eye = (down == lax.broadcasted_iota(jnp.int32, (rank, rank), 1)).astype(F32)
    rest = jnp.concatenate([gram, eye], axis=1)
    done = []
    for p in range(0, rank, size):
        top, rest = rest[:size], rest[size:]
        panel = [top[8 * t:8 * t + 8] for t in range(tiles)]
        cols = [[jnp.broadcast_to(panel[t][:, p + k:p + k + 1], (8, rank)) if t >= k // 8 else None
                 for t in range(tiles)] for k in range(size)]
        pivots = [jnp.zeros((8, rank), F32) for _ in range(tiles)]
        for k in range(size):
            at, row = k // 8, k % 8
            pivot = cols[k][at][row:row + 1, :]
            pivots[at] = jnp.where(line == row, pivot, pivots[at])
            if k == size - 1:
                break
            over = 1.0 / pivot
            head = panel[at][row:row + 1, :]
            for t in range(at, tiles):
                factor = cols[k][t] * over
                if t == at:
                    factor = jnp.where(line > row, factor, 0.0)
                for l in range(k + 1, 8 * t + 8):
                    cols[l][t] = cols[l][t] - factor * cols[k][l // 8][l % 8:l % 8 + 1, :]
                panel[t] = panel[t] - jnp.concatenate([factor, factor], axis=1) * head
        scaled = jnp.concatenate(pivots, axis=0)
        full = jnp.concatenate(panel, axis=0)
        done.append(full[:, rank:] * lax.rsqrt(scaled))
        if p + size < rank:
            weights = full[:, :rank] * (1.0 / scaled)
            rest = rest - across_rows(weights[:, p + size:], full)
    return jnp.concatenate(done, axis=0)


def partner(index, step):
    return (index, index + 1 - 2 * lax.rem(index, 2), lax.rem(index + 2, 4), 3 - index)[step]


HOPS = (3, 2, 1)
NT = (((1,), (1,)), ((), ()))


def range_kernel(cuts, group_of, windows, sketches, basis, projection,
                 held0, held1, held2, held3, stage, taken, pieces, block, kernel_rows, part1, part2, rs1, rs2, sk, power,
                 in_sem, om_sem, a_send, a_recv, f_send, f_recv,
                 s1_send, s1_recv, g1_send, g1_recv, h1_send, h1_recv,
                 s2_send, s2_recv, g2_send, g2_recv, h2_send, h2_recv):
    g, r, c = lax.axis_index("grp"), lax.axis_index("row"), lax.axis_index("col")
    height = windows.shape[1]
    rows, wide = block.shape
    deep, share = rows // 2, rows // 8
    root = math.sqrt(rows)
    other = (g, 1 - r, c)

    def columns(z):
        return pl.ds(pl.multiple_of(z * wide, 128), wide)

    held = (held0, held1, held2, held3)
    loads = {}
    for dz in (2, 3, 1, 0):
        loads[dz] = pltpu.make_async_copy(
            windows.at[:, :, columns(partner(c, dz))], held[dz], in_sem.at[dz])
        loads[dz].start()
    barrier = pltpu.get_barrier_semaphore()
    for dz in range(4):
        for dg in range(4):
            if dz or dg:
                pl.semaphore_signal(barrier, inc=1, device_id=(partner(g, dg), r, partner(c, dz)),
                                    device_id_type=MESH)
    pl.semaphore_signal(barrier, inc=1, device_id=other, device_id_type=MESH)

    def owner(slot):
        found = jnp.int32(0)
        for m in range(4):
            found = jnp.where(group_of[m] == slot, jnp.int32(m), found)
        return found

    sources = [owner(partner(g, dg)) for dg in range(4)]
    across_order = [(dz, dg) for dg in range(4) for dz in (2, 3)]
    near_order = [(dz, dg) for dz in (1, 0) for dg in (3, 1, 2, 0)]

    sends = {}

    def send(dz, dg):
        copy = pltpu.make_async_remote_copy(
            src_ref=stage.at[dz, dg], dst_ref=pieces.at[r, g, c],
            send_sem=a_send.at[dz, dg], recv_sem=a_recv.at[dz, dg],
            device_id=(partner(g, dg), r, partner(c, dz)), device_id_type=MESH)
        copy.start()
        sends[dz, dg] = copy

    for dz in (2, 3, 1, 0):
        loads[dz].wait()
        for dg in range(4):
            if dz or dg:
                stage[dz, dg] = held[dz][sources[dg]]
            else:
                pieces[r, g, c] = held[0][sources[0]]
        if dz == 3:
            pl.semaphore_wait(barrier, 16)
            for dz_, dg in across_order:
                send(dz_, dg)
    for dz, dg in near_order:
        if dz or dg:
            send(dz, dg)
    load_omega = pltpu.make_async_copy(sketches, taken, om_sem)
    load_omega.start()
    load_omega.wait()
    omega = taken[sources[0]]

    forwards = {}

    def forward(dz, dg):
        spot = pieces.at[r, partner(g, dg), partner(c, dz)]
        copy = pltpu.make_async_remote_copy(
            src_ref=spot, dst_ref=spot, send_sem=f_send.at[dz, dg], recv_sem=f_recv.at[dz, dg],
            device_id=other, device_id_type=MESH)
        copy.start()
        forwards[dz, dg] = copy

    def pair_rows(side, dg, far):
        half = lax.rem(c // 2 + far, 2)
        start = ((side * 4 + partner(g, dg)) * 4 + 2 * half) * height
        return half, pl.ds(pl.multiple_of(start, 16), 2 * height)

    def settle(side, dg, far):
        half, place = pair_rows(side, dg, far)
        block[place, :] = pieces[side, partner(g, dg), pl.ds(2 * half, 2)].reshape(2 * height, wide)
        return half, place

    def sketch(dg, far):
        half, place = settle(r, dg, far)
        done = jnp.dot(block[place, :], omega, preferred_element_type=F32)
        into = pl.ds(pl.multiple_of(2 * height * half, 16), 2 * height)
        part1[partner(g, dg), into, :] = done.astype(BF16)

    pairs = [(dg, 0) for dg in (3, 1, 2, 0)] + [(dg, 1) for dg in range(4)]
    for i, (dg, far) in enumerate(pairs):
        for dz in ((0, 1), (2, 3))[far]:
            if dz or dg:
                sends[dz, dg].wait_recv()
            forward(dz, dg)
        if i:
            before = pairs[i - 1]
            for dz in ((0, 1), (2, 3))[before[1]]:
                forwards[dz, before[0]].wait_recv()
            settle(1 - r, *before)
        sketch(dg, far)

    def scatter(part, rs, send_sem, recv_sem):
        copies = []
        for dz in HOPS:
            k = partner(c, dz)
            copy = pltpu.make_async_remote_copy(
                src_ref=part.at[k], dst_ref=rs.at[dz], send_sem=send_sem.at[dz],
                recv_sem=recv_sem.at[dz], device_id=(g, r, k), device_id_type=MESH)
            copy.start()
            copies.append(copy)
        return copies

    def total(part, rs, copies):
        for copy in copies:
            copy.wait()
        found = part[c].astype(F32)
        for dz in HOPS:
            found = found + rs[dz].astype(F32)
        return found

    def gather(ref, g_send, g_recv, h_send, h_recv):
        def spot(k):
            return ref.at[pl.ds(pl.multiple_of(r * deep + k * share, 16), share), :]

        copies, passed = [], []

        def hand(dz):
            place = spot(partner(c, dz))
            copy = pltpu.make_async_remote_copy(
                src_ref=place, dst_ref=place, send_sem=h_send.at[dz], recv_sem=h_recv.at[dz],
                device_id=other, device_id_type=MESH)
            copy.start()
            passed.append(copy)

        for dz in HOPS:
            copy = pltpu.make_async_remote_copy(
                src_ref=spot(c), dst_ref=spot(c), send_sem=g_send.at[dz], recv_sem=g_recv.at[dz],
                device_id=(g, r, partner(c, dz)), device_id_type=MESH)
            copy.start()
            copies.append((dz, copy))
        hand(0)
        def finish():
            for dz, copy in reversed(copies):
                copy.wait_recv()
                hand(dz)
            for _, copy in copies:
                copy.wait_send()
            for copy in passed:
                copy.wait()
        return finish

    def own_rows(side):
        return pl.ds(pl.multiple_of(side * deep, 16), deep)

    copies = scatter(part1, rs1, s1_send, s1_recv)

    def kernel_block(side):
        found = lax.dot_general(block[own_rows(r), :], block[own_rows(side), :], NT,
                                preferred_element_type=F32)
        kernel_rows[side] = found.astype(BF16)

    kernel_block(r)
    sk[pl.ds(pl.multiple_of(r * deep + c * share, 16), share), :] = total(
        part1, rs1, copies).astype(BF16)
    finish = gather(sk, g1_send, g1_recv, h1_send, h1_recv)
    last = pairs[-1]
    for dz in (2, 3):
        forwards[dz, last[0]].wait_recv()
    settle(1 - r, *last)
    kernel_block(1 - r)
    finish()

    found = (jnp.dot(kernel_rows[0], sk[:deep, :], preferred_element_type=F32)
             + jnp.dot(kernel_rows[1], sk[deep:, :], preferred_element_type=F32))
    for k in range(4):
        part2[k] = found[k * share:(k + 1) * share, :].astype(BF16)
    mine = total(part2, rs2, scatter(part2, rs2, s2_send, s2_recv))
    power[pl.ds(pl.multiple_of(r * deep + c * share, 16), share), :] = mine.astype(BF16)
    gather(power, g2_send, g2_recv, h2_send, h2_recv)()

    whole = power[...]
    gram = lax.dot_general(whole, whole, (((0,), (0,)), ((), ())), preferred_element_type=F32)
    inverse = inverse_factor(gram, 32)
    parts = thirds(inverse * root)
    found = lax.dot_general(jnp.concatenate(parts, axis=0), whole, NT, preferred_element_type=F32)
    rank = inverse.shape[0]
    turned = (found[2 * rank:] + found[rank:2 * rank] + found[:rank]).astype(BF16)
    step = wide // cuts
    scale = math.sqrt(4 * wide / rows)
    for i in range(cuts):
        span = pl.ds(i * step, step)
        projection[:, span] = jnp.dot(turned, block[:, span], preferred_element_type=F32) * scale
    basis[...] = lax.dot_general(mine, inverse, NT, precision=lax.Precision.HIGHEST,
                                 preferred_element_type=F32) * root
    for copy in sends.values():
        copy.wait_send()
    for copy in forwards.values():
        copy.wait_send()


def write_kernel(basis, projection, basis_out, projection_out, basis_sem, projection_sem):
    first = pltpu.make_async_copy(projection, projection_out.at[0], projection_sem)
    first.start()
    second = pltpu.make_async_copy(basis, basis_out.at[0], basis_sem)
    second.start()
    first.wait()
    second.wait()


def fused_device(layer_windows, sketches, group_of):
    _, height, total_cols = layer_windows.shape
    rank = sketches.shape[2]
    wide = total_cols // 4
    rows = height * 32
    share = rows // 8
    cuts = 8
    vmem = pl.BlockSpec(memory_space=pltpu.VMEM)
    hbm = pl.BlockSpec(memory_space=pltpu.HBM)
    dma = pltpu.SemaphoreType.DMA
    basis, projection = pl.pallas_call(
        functools.partial(range_kernel, cuts),
        out_shape=(
            jax.ShapeDtypeStruct((share, rank), F32),
            jax.ShapeDtypeStruct((rank, wide), F32),
        ),
        in_specs=[pl.BlockSpec(memory_space=pltpu.SMEM), hbm, hbm],
        out_specs=(vmem, vmem),
        scratch_shapes=[
            *[pltpu.VMEM((4, height, wide), BF16)] * 4,
            pltpu.VMEM((4, 4, height, wide), BF16),
            pltpu.VMEM(sketches.shape, BF16),
            pltpu.VMEM((2, 4, 4, height, wide), BF16),
            pltpu.VMEM((rows, wide), BF16),
            pltpu.VMEM((2, rows // 2, rows // 2), BF16),
            pltpu.VMEM((4, share, rank), BF16),
            pltpu.VMEM((4, share, rank), BF16),
            pltpu.VMEM((4, share, rank), BF16),
            pltpu.VMEM((4, share, rank), BF16),
            pltpu.VMEM((rows, rank), BF16),
            pltpu.VMEM((rows, rank), BF16),
            dma((4,)), dma,
            dma((4, 4)), dma((4, 4)), dma((4, 4)), dma((4, 4)),
            dma((4,)), dma((4,)), dma((4,)), dma((4,)), dma((4,)), dma((4,)),
            dma((4,)), dma((4,)), dma((4,)), dma((4,)), dma((4,)), dma((4,)),
        ],
        compiler_params=pltpu.CompilerParams(
            collective_id=0, has_side_effects=True, vmem_limit_bytes=50 << 20),
        name="range_finder",
    )(group_of, layer_windows, sketches)
    return pl.pallas_call(
        write_kernel,
        out_shape=(
            jax.ShapeDtypeStruct((1, share, rank), F32),
            jax.ShapeDtypeStruct((1, rank, wide), F32),
        ),
        in_specs=[vmem, vmem],
        out_specs=(hbm, hbm),
        scratch_shapes=[dma, dma],
        compiler_params=pltpu.CompilerParams(vmem_limit_bytes=8 << 20),
        name="write_out",
    )(basis, projection)


def solution(mesh):
    in_specs = (P(None, ("row", "grp", "col"), None), P(None, "col", None), P())
    out_specs = (P("grp", ("row", "col"), None), P("grp", None, "col"))
    sizes = (mesh.shape["grp"], mesh.shape["row"], mesh.shape["col"])

    def body(layer_windows, sketches, group_of):
        count, height, total_cols = layer_windows.shape
        fits = sizes == (4, 2, 4) and count == 4 and height % 8 == 0 and height <= 32
        if fits and sketches.shape[2] == 128 and total_cols in (8192, 16384):
            return fused_device(layer_windows, sketches, group_of)
        return per_device(layer_windows, sketches, group_of)

    return jax.shard_map(body, mesh=mesh, in_specs=in_specs, out_specs=out_specs, check_vma=False)
```

```python
import functools
import math

import jax
import jax.numpy as jnp
from jax import lax
from jax.experimental import pallas as pl
from jax.experimental.pallas import tpu as pltpu
from jax.sharding import PartitionSpec as P

MESH = pl.DeviceIdType.MESH
F32 = jnp.float32
BF16 = jnp.bfloat16


def across(left, right):
    return lax.dot_general(
        left, right, (((0,), (0,)), ((), ())), preferred_element_type=jnp.float32
    )


def right_solve(lower, power):
    return lax.linalg.triangular_solve(lower, power, left_side=False, lower=True, transpose_a=True)


def owners(group_of):
    count = group_of.shape[0]
    slots = jnp.arange(count, dtype=jnp.int32)
    matched = (group_of[None, :] == slots[:, None]).astype(jnp.int32)
    return jnp.sum(matched * slots[None, :], axis=1)


def per_device(layer_windows, sketches, group_of):
    owner_of = owners(group_of)
    ordered = jnp.stack([
        lax.dynamic_index_in_dim(layer_windows, owner_of[j], 0, keepdims=False)
        for j in range(layer_windows.shape[0])
    ])
    block = lax.all_to_all(
        lax.all_to_all(ordered, "col", split_axis=2, concat_axis=1, tiled=True),
        "grp",
        split_axis=0,
        concat_axis=1,
        tiled=True,
    )[0]
    mine = owner_of[lax.axis_index("grp")]
    omega = lax.dynamic_index_in_dim(sketches, mine, 0, keepdims=False)
    total_rows = block.shape[0] * lax.axis_size("row")
    total_cols = block.shape[1] * lax.axis_size("col")
    share = block.shape[0] // lax.axis_size("col")

    def summed_rows(right):
        return lax.psum(jnp.dot(block, right, preferred_element_type=jnp.float32), "col")

    sketched = summed_rows(omega).astype(jnp.bfloat16)
    back = lax.psum(across(block, sketched).astype(jnp.bfloat16), "row")
    power = summed_rows(back)
    gram = lax.psum(
        jnp.dot(power.T, power, precision=lax.Precision.HIGHEST).astype(jnp.bfloat16), "row"
    ).astype(jnp.float32)
    lower = jnp.linalg.cholesky(gram)
    ortho = right_solve(lower, power) * math.sqrt(total_rows)
    basis_share = lax.dynamic_slice_in_dim(ortho, lax.axis_index("col") * share, share, 0)
    ortho_low = ortho.astype(jnp.bfloat16)
    projected = lax.psum(across(ortho_low, block).astype(jnp.bfloat16), "row").astype(
        jnp.float32
    ) * math.sqrt(total_cols / total_rows)
    return (basis_share[None], projected[None])


def thirds(array):
    high = array.astype(BF16)
    rest = array - high.astype(F32)
    middle = rest.astype(BF16)
    return high, middle, (rest - middle.astype(F32)).astype(BF16)


def across_rows(left, right):
    a, b, c = thirds(left)
    d, e, f = thirds(right)
    return lax.dot_general(
        jnp.concatenate([a, a, b, a, b, c], axis=0), jnp.concatenate([d, e, d, f, e, d], axis=0),
        (((0,), (0,)), ((), ())), preferred_element_type=F32)


def inverse_factor(gram, size, between):
    rank = gram.shape[0]
    tiles = size // 8
    line = lax.broadcasted_iota(jnp.int32, (8, rank), 0)
    down = lax.broadcasted_iota(jnp.int32, (rank, rank), 0)
    eye = (down == lax.broadcasted_iota(jnp.int32, (rank, rank), 1)).astype(F32)
    rest = jnp.concatenate([gram, eye], axis=1)
    done = []
    for p in range(0, rank, size):
        top, rest = rest[:size], rest[size:]
        panel = [top[8 * t:8 * t + 8] for t in range(tiles)]
        cols = [[jnp.broadcast_to(panel[t][:, p + k:p + k + 1], (8, rank)) if t >= k // 8 else None
                 for t in range(tiles)] for k in range(size)]
        pivots = [jnp.zeros((8, rank), F32) for _ in range(tiles)]
        for k in range(size):
            at, row = k // 8, k % 8
            pivot = cols[k][at][row:row + 1, :]
            pivots[at] = jnp.where(line == row, pivot, pivots[at])
            if k == size - 1:
                break
            over = 1.0 / pivot
            head = panel[at][row:row + 1, :]
            for t in range(at, tiles):
                factor = cols[k][t] * over
                if t == at:
                    factor = jnp.where(line > row, factor, 0.0)
                for l in range(k + 1, 8 * t + 8):
                    cols[l][t] = cols[l][t] - factor * cols[k][l // 8][l % 8:l % 8 + 1, :]
                panel[t] = panel[t] - jnp.concatenate([factor, factor], axis=1) * head
        scaled = jnp.concatenate(pivots, axis=0)
        full = jnp.concatenate(panel, axis=0)
        done.append(full[:, rank:] * lax.rsqrt(scaled))
        between(p // size)
        if p + size < rank:
            weights = full[:, :rank] * (1.0 / scaled)
            rest = rest - across_rows(weights[:, p + size:], full)
    return jnp.concatenate(done, axis=0)


def partner(index, step):
    return (index, index + 1 - 2 * lax.rem(index, 2), lax.rem(index + 2, 4), 3 - index)[step]


HOPS = (3, 2, 1)
NT = (((1,), (1,)), ((), ()))


def range_kernel(group_of, windows, sketches, own_power, factor_out, high_out, low_out, tall,
                 held0, held1, held2, held3, stage, taken, pieces, block, kernel_rows, part1, part2, rs1, rs2, sk, power,
                 in_sem, om_sem, a_send, a_recv, f_send, f_recv,
                 s1_send, s1_recv, g1_send, g1_recv, h1_send, h1_recv,
                 s2_send, s2_recv, g2_send, g2_recv, h2_send, h2_recv):
    g, r, c = lax.axis_index("grp"), lax.axis_index("row"), lax.axis_index("col")
    height = windows.shape[1]
    rows, wide = block.shape
    deep, share = rows // 2, rows // 8
    other = (g, 1 - r, c)

    def columns(z):
        return pl.ds(pl.multiple_of(z * wide, 128), wide)

    held = (held0, held1, held2, held3)
    loads = {}
    for dz in (2, 3, 1, 0):
        loads[dz] = pltpu.make_async_copy(
            windows.at[:, :, columns(partner(c, dz))], held[dz], in_sem.at[dz])
        loads[dz].start()
    barrier = pltpu.get_barrier_semaphore()
    for dz in range(4):
        for dg in range(4):
            if dz or dg:
                pl.semaphore_signal(barrier, inc=1, device_id=(partner(g, dg), r, partner(c, dz)),
                                    device_id_type=MESH)
    pl.semaphore_signal(barrier, inc=1, device_id=other, device_id_type=MESH)

    def owner(slot):
        found = jnp.int32(0)
        for m in range(4):
            found = jnp.where(group_of[m] == slot, jnp.int32(m), found)
        return found

    sources = [owner(partner(g, dg)) for dg in range(4)]
    across_order = [(dz, dg) for dg in range(4) for dz in (2, 3)]
    near_order = [(dz, dg) for dz in (1, 0) for dg in (3, 1, 2, 0)]

    sends = {}

    def send(dz, dg):
        copy = pltpu.make_async_remote_copy(
            src_ref=stage.at[dz, dg], dst_ref=pieces.at[r, g, c],
            send_sem=a_send.at[dz, dg], recv_sem=a_recv.at[dz, dg],
            device_id=(partner(g, dg), r, partner(c, dz)), device_id_type=MESH)
        copy.start()
        sends[dz, dg] = copy

    for dz in (2, 3, 1, 0):
        loads[dz].wait()
        for dg in range(4):
            if dz or dg:
                stage[dz, dg] = held[dz][sources[dg]]
            else:
                pieces[r, g, c] = held[0][sources[0]]
        if dz == 3:
            pl.semaphore_wait(barrier, 16)
            for dz_, dg in across_order:
                send(dz_, dg)
    for dz, dg in near_order:
        if dz or dg:
            send(dz, dg)
    load_omega = pltpu.make_async_copy(sketches, taken, om_sem)
    load_omega.start()
    load_omega.wait()
    omega = taken[sources[0]]

    forwards = {}

    def forward(dz, dg):
        spot = pieces.at[r, partner(g, dg), partner(c, dz)]
        copy = pltpu.make_async_remote_copy(
            src_ref=spot, dst_ref=spot, send_sem=f_send.at[dz, dg], recv_sem=f_recv.at[dz, dg],
            device_id=other, device_id_type=MESH)
        copy.start()
        forwards[dz, dg] = copy

    def pair_rows(side, dg, far):
        half = lax.rem(c // 2 + far, 2)
        start = ((side * 4 + partner(g, dg)) * 4 + 2 * half) * height
        return half, pl.ds(pl.multiple_of(start, 16), 2 * height)

    def settle(side, dg, far):
        half, place = pair_rows(side, dg, far)
        block[place, :] = pieces[side, partner(g, dg), pl.ds(2 * half, 2)].reshape(2 * height, wide)
        return half, place

    def sketch(dg, far):
        half, place = settle(r, dg, far)
        done = jnp.dot(block[place, :], omega, preferred_element_type=F32)
        into = pl.ds(pl.multiple_of(2 * height * half, 16), 2 * height)
        part1[partner(g, dg), into, :] = done.astype(BF16)

    pairs = [(dg, 0) for dg in (3, 1, 2, 0)] + [(dg, 1) for dg in range(4)]
    for i, (dg, far) in enumerate(pairs):
        for dz in ((0, 1), (2, 3))[far]:
            if dz or dg:
                sends[dz, dg].wait_recv()
            forward(dz, dg)
        if i:
            before = pairs[i - 1]
            for dz in ((0, 1), (2, 3))[before[1]]:
                forwards[dz, before[0]].wait_recv()
            settle(1 - r, *before)
        sketch(dg, far)

    def scatter(part, rs, send_sem, recv_sem):
        copies = []
        for dz in HOPS:
            k = partner(c, dz)
            copy = pltpu.make_async_remote_copy(
                src_ref=part.at[k], dst_ref=rs.at[dz], send_sem=send_sem.at[dz],
                recv_sem=recv_sem.at[dz], device_id=(g, r, k), device_id_type=MESH)
            copy.start()
            copies.append(copy)
        return copies

    def total(part, rs, copies):
        for copy in copies:
            copy.wait()
        found = part[c].astype(F32)
        for dz in HOPS:
            found = found + rs[dz].astype(F32)
        return found

    def gather(ref, g_send, g_recv, h_send, h_recv):
        def spot(k):
            return ref.at[pl.ds(pl.multiple_of(r * deep + k * share, 16), share), :]

        copies, passed = [], []

        def hand(dz):
            place = spot(partner(c, dz))
            copy = pltpu.make_async_remote_copy(
                src_ref=place, dst_ref=place, send_sem=h_send.at[dz], recv_sem=h_recv.at[dz],
                device_id=other, device_id_type=MESH)
            copy.start()
            passed.append(copy)

        for dz in HOPS:
            copy = pltpu.make_async_remote_copy(
                src_ref=spot(c), dst_ref=spot(c), send_sem=g_send.at[dz], recv_sem=g_recv.at[dz],
                device_id=(g, r, partner(c, dz)), device_id_type=MESH)
            copy.start()
            copies.append((dz, copy))
        hand(0)
        def finish():
            for dz, copy in reversed(copies):
                copy.wait_recv()
                hand(dz)
            for _, copy in copies:
                copy.wait_send()
            for copy in passed:
                copy.wait()
        return finish

    def own_rows(side):
        return pl.ds(pl.multiple_of(side * deep, 16), deep)

    copies = scatter(part1, rs1, s1_send, s1_recv)

    def kernel_block(side):
        found = lax.dot_general(block[own_rows(r), :], block[own_rows(side), :], NT,
                                preferred_element_type=F32)
        kernel_rows[side] = found.astype(BF16)

    kernel_block(r)
    sk[pl.ds(pl.multiple_of(r * deep + c * share, 16), share), :] = total(
        part1, rs1, copies).astype(BF16)
    finish = gather(sk, g1_send, g1_recv, h1_send, h1_recv)
    last = pairs[-1]
    for dz in (2, 3):
        forwards[dz, last[0]].wait_recv()
    settle(1 - r, *last)
    kernel_block(1 - r)
    finish()

    found = (jnp.dot(kernel_rows[0], sk[:deep, :], preferred_element_type=F32)
             + jnp.dot(kernel_rows[1], sk[deep:, :], preferred_element_type=F32))
    for k in range(4):
        part2[k] = found[k * share:(k + 1) * share, :].astype(BF16)
    mine = total(part2, rs2, scatter(part2, rs2, s2_send, s2_recv))
    power[pl.ds(pl.multiple_of(r * deep + c * share, 16), share), :] = mine.astype(BF16)
    own_power[...] = mine
    gather(power, g2_send, g2_recv, h2_send, h2_recv)()

    whole = power[...]
    gram = lax.dot_general(whole, whole, (((0,), (0,)), ((), ())), preferred_element_type=F32)
    tall[...] = whole.astype(F32).T.astype(BF16)
    step = wide // 4

    def weigh(i):
        span = pl.ds(i * step, step)
        found = jnp.dot(tall[...], block[:, span], preferred_element_type=F32)
        high = found.astype(BF16)
        high_out[:, span] = high
        low_out[:, span] = (found - high.astype(F32)).astype(BF16)

    inverse = inverse_factor(gram, 32, weigh)
    factor_out[...] = inverse
    for copy in sends.values():
        copy.wait_send()
    for copy in forwards.values():
        copy.wait_send()


def project_kernel(cuts, own_power, factor, high, low, basis_out, projection,
                   shown, basis, basis_sem, out_sem):
    rank, wide = high.shape
    step = wide // cuts
    scaled = factor[...] * math.sqrt(4 * wide)
    above = scaled.astype(BF16)
    both = jnp.concatenate([above, (scaled - above.astype(F32)).astype(BF16)], axis=0)
    copies = []
    for i in range(cuts):
        span = pl.ds(i * step, step)
        found = jnp.dot(both, high[:, span], preferred_element_type=F32)
        small = jnp.dot(above, low[:, span], preferred_element_type=F32)
        shown[:, span] = found[:rank] + (found[rank:] + small)
        copy = pltpu.make_async_copy(shown.at[:, span], projection.at[0, :, span], out_sem.at[i])
        copy.start()
        copies.append(copy)
        if i == cuts // 2:
            basis[...] = lax.dot_general(
                own_power[...], factor[...], NT, precision=lax.Precision.HIGHEST,
                preferred_element_type=F32) * math.sqrt(8 * own_power.shape[0])
            last = pltpu.make_async_copy(basis, basis_out.at[0], basis_sem)
            last.start()
            copies.append(last)
    for copy in copies:
        copy.wait()


def fused_device(layer_windows, sketches, group_of):
    _, height, total_cols = layer_windows.shape
    rank = sketches.shape[2]
    wide = total_cols // 4
    rows = height * 32
    share = rows // 8
    cuts = 8
    vmem = pl.BlockSpec(memory_space=pltpu.VMEM)
    hbm = pl.BlockSpec(memory_space=pltpu.HBM)
    dma = pltpu.SemaphoreType.DMA
    own_power, factor, high, low = pl.pallas_call(
        range_kernel,
        out_shape=(
            jax.ShapeDtypeStruct((share, rank), F32),
            jax.ShapeDtypeStruct((rank, rank), F32),
            jax.ShapeDtypeStruct((rank, wide), BF16),
            jax.ShapeDtypeStruct((rank, wide), BF16),
        ),
        in_specs=[pl.BlockSpec(memory_space=pltpu.SMEM), hbm, hbm],
        out_specs=(vmem,) * 4,
        scratch_shapes=[
            pltpu.VMEM((rank, rows), BF16),
            *[pltpu.VMEM((4, height, wide), BF16)] * 4,
            pltpu.VMEM((4, 4, height, wide), BF16),
            pltpu.VMEM(sketches.shape, BF16),
            pltpu.VMEM((2, 4, 4, height, wide), BF16),
            pltpu.VMEM((rows, wide), BF16),
            pltpu.VMEM((2, rows // 2, rows // 2), BF16),
            pltpu.VMEM((4, share, rank), BF16),
            pltpu.VMEM((4, share, rank), BF16),
            pltpu.VMEM((4, share, rank), BF16),
            pltpu.VMEM((4, share, rank), BF16),
            pltpu.VMEM((rows, rank), BF16),
            pltpu.VMEM((rows, rank), BF16),
            dma((4,)), dma,
            dma((4, 4)), dma((4, 4)), dma((4, 4)), dma((4, 4)),
            dma((4,)), dma((4,)), dma((4,)), dma((4,)), dma((4,)), dma((4,)),
            dma((4,)), dma((4,)), dma((4,)), dma((4,)), dma((4,)), dma((4,)),
        ],
        compiler_params=pltpu.CompilerParams(
            collective_id=0, has_side_effects=True, vmem_limit_bytes=50 << 20),
        name="range_finder",
    )(group_of, layer_windows, sketches)
    return pl.pallas_call(
        functools.partial(project_kernel, cuts),
        out_shape=(
            jax.ShapeDtypeStruct((1, share, rank), F32),
            jax.ShapeDtypeStruct((1, rank, wide), F32),
        ),
        in_specs=[vmem] * 4,
        out_specs=(hbm, hbm),
        scratch_shapes=[pltpu.VMEM((rank, wide), F32), pltpu.VMEM((share, rank), F32), dma, dma((cuts,))],
        compiler_params=pltpu.CompilerParams(vmem_limit_bytes=8 << 20),
        name="project",
    )(own_power, factor, high, low)


def solution(mesh):
    in_specs = (P(None, ("row", "grp", "col"), None), P(None, "col", None), P())
    out_specs = (P("grp", ("row", "col"), None), P("grp", None, "col"))
    sizes = (mesh.shape["grp"], mesh.shape["row"], mesh.shape["col"])

    def body(layer_windows, sketches, group_of):
        count, height, total_cols = layer_windows.shape
        fits = sizes == (4, 2, 4) and count == 4 and height % 8 == 0 and height <= 32
        if fits and sketches.shape[2] == 128 and total_cols in (8192, 16384):
            return fused_device(layer_windows, sketches, group_of)
        return per_device(layer_windows, sketches, group_of)

    return jax.shard_map(body, mesh=mesh, in_specs=in_specs, out_specs=out_specs, check_vma=False)
```

```python
import functools
import math

import jax
import jax.numpy as jnp
from jax import lax
from jax.experimental import pallas as pl
from jax.experimental.pallas import tpu as pltpu
from jax.sharding import PartitionSpec as P

MESH = pl.DeviceIdType.MESH
F32 = jnp.float32
BF16 = jnp.bfloat16


def across(left, right):
    return lax.dot_general(
        left, right, (((0,), (0,)), ((), ())), preferred_element_type=jnp.float32
    )


def right_solve(lower, power):
    return lax.linalg.triangular_solve(lower, power, left_side=False, lower=True, transpose_a=True)


def owners(group_of):
    count = group_of.shape[0]
    slots = jnp.arange(count, dtype=jnp.int32)
    matched = (group_of[None, :] == slots[:, None]).astype(jnp.int32)
    return jnp.sum(matched * slots[None, :], axis=1)


def per_device(layer_windows, sketches, group_of):
    owner_of = owners(group_of)
    ordered = jnp.stack([
        lax.dynamic_index_in_dim(layer_windows, owner_of[j], 0, keepdims=False)
        for j in range(layer_windows.shape[0])
    ])
    block = lax.all_to_all(
        lax.all_to_all(ordered, "col", split_axis=2, concat_axis=1, tiled=True),
        "grp",
        split_axis=0,
        concat_axis=1,
        tiled=True,
    )[0]
    mine = owner_of[lax.axis_index("grp")]
    omega = lax.dynamic_index_in_dim(sketches, mine, 0, keepdims=False)
    total_rows = block.shape[0] * lax.axis_size("row")
    total_cols = block.shape[1] * lax.axis_size("col")
    share = block.shape[0] // lax.axis_size("col")

    def summed_rows(right):
        return lax.psum(jnp.dot(block, right, preferred_element_type=jnp.float32), "col")

    sketched = summed_rows(omega).astype(jnp.bfloat16)
    back = lax.psum(across(block, sketched).astype(jnp.bfloat16), "row")
    power = summed_rows(back)
    gram = lax.psum(
        jnp.dot(power.T, power, precision=lax.Precision.HIGHEST).astype(jnp.bfloat16), "row"
    ).astype(jnp.float32)
    lower = jnp.linalg.cholesky(gram)
    ortho = right_solve(lower, power) * math.sqrt(total_rows)
    basis_share = lax.dynamic_slice_in_dim(ortho, lax.axis_index("col") * share, share, 0)
    ortho_low = ortho.astype(jnp.bfloat16)
    projected = lax.psum(across(ortho_low, block).astype(jnp.bfloat16), "row").astype(
        jnp.float32
    ) * math.sqrt(total_cols / total_rows)
    return (basis_share[None], projected[None])


def thirds(array):
    high = array.astype(BF16)
    rest = array - high.astype(F32)
    middle = rest.astype(BF16)
    return high, middle, (rest - middle.astype(F32)).astype(BF16)


def across_rows(left, right):
    a, b, c = thirds(left)
    d, e, f = thirds(right)
    return lax.dot_general(
        jnp.concatenate([a, a, b, a, b, c], axis=0), jnp.concatenate([d, e, d, f, e, d], axis=0),
        (((0,), (0,)), ((), ())), preferred_element_type=F32)


def inverse_factor(gram, size, between):
    rank = gram.shape[0]
    tiles = size // 8
    line = lax.broadcasted_iota(jnp.int32, (8, rank), 0)
    down = lax.broadcasted_iota(jnp.int32, (rank, rank), 0)
    eye = (down == lax.broadcasted_iota(jnp.int32, (rank, rank), 1)).astype(F32)
    rest = jnp.concatenate([gram, eye], axis=1)
    done = []
    for p in range(0, rank, size):
        top, rest = rest[:size], rest[size:]
        panel = [top[8 * t:8 * t + 8] for t in range(tiles)]
        cols = [[jnp.broadcast_to(panel[t][:, p + k:p + k + 1], (8, rank)) if t >= k // 8 else None
                 for t in range(tiles)] for k in range(size)]
        pivots = [jnp.zeros((8, rank), F32) for _ in range(tiles)]
        for k in range(size):
            at, row = k // 8, k % 8
            pivot = cols[k][at][row:row + 1, :]
            pivots[at] = jnp.where(line == row, pivot, pivots[at])
            if k == size - 1:
                break
            over = 1.0 / pivot
            head = panel[at][row:row + 1, :]
            for t in range(at, tiles):
                factor = cols[k][t] * over
                if t == at:
                    factor = jnp.where(line > row, factor, 0.0)
                for l in range(k + 1, 8 * t + 8):
                    cols[l][t] = cols[l][t] - factor * cols[k][l // 8][l % 8:l % 8 + 1, :]
                panel[t] = panel[t] - jnp.concatenate([factor, factor], axis=1) * head
        scaled = jnp.concatenate(pivots, axis=0)
        full = jnp.concatenate(panel, axis=0)
        done.append(full[:, rank:] * lax.rsqrt(scaled))
        between(p // size)
        if p + size < rank:
            weights = full[:, :rank] * (1.0 / scaled)
            rest = rest - across_rows(weights[:, p + size:], full)
    return jnp.concatenate(done, axis=0)


def partner(index, step):
    return (index, index + 1 - 2 * lax.rem(index, 2), lax.rem(index + 2, 4), 3 - index)[step]


HOPS = (2, 3, 1)
NT = (((1,), (1,)), ((), ()))


def range_kernel(group_of, windows, sketches, own_power, factor_out, high_out, low_out, tall,
                 held0, held1, held2, held3, stage, taken, pieces, block, kernel_rows, part1, part2, rs1, rs2, sk, power,
                 in_sem, om_sem, a_send, a_recv, f_send, f_recv,
                 s1_send, s1_recv, g1_send, g1_recv, h1_send, h1_recv,
                 s2_send, s2_recv, g2_send, g2_recv, h2_send, h2_recv):
    g, r, c = lax.axis_index("grp"), lax.axis_index("row"), lax.axis_index("col")
    height = windows.shape[1]
    rows, wide = block.shape
    deep, share = rows // 2, rows // 8
    other = (g, 1 - r, c)

    def columns(z):
        return pl.ds(pl.multiple_of(z * wide, 128), wide)

    held = (held0, held1, held2, held3)
    loads = {}
    for dz in (2, 3, 1, 0):
        loads[dz] = pltpu.make_async_copy(
            windows.at[:, :, columns(partner(c, dz))], held[dz], in_sem.at[dz])
        loads[dz].start()
    barrier = pltpu.get_barrier_semaphore()
    for dz in range(4):
        for dg in range(4):
            if dz or dg:
                pl.semaphore_signal(barrier, inc=1, device_id=(partner(g, dg), r, partner(c, dz)),
                                    device_id_type=MESH)
    pl.semaphore_signal(barrier, inc=1, device_id=other, device_id_type=MESH)

    def owner(slot):
        found = jnp.int32(0)
        for m in range(4):
            found = jnp.where(group_of[m] == slot, jnp.int32(m), found)
        return found

    sources = [owner(partner(g, dg)) for dg in range(4)]
    across_order = [(dz, dg) for dg in range(4) for dz in (2, 3)]
    near_order = [(dz, dg) for dz in (1, 0) for dg in (3, 1, 2, 0)]

    sends = {}

    def send(dz, dg):
        copy = pltpu.make_async_remote_copy(
            src_ref=stage.at[dz, dg], dst_ref=pieces.at[r, g, c],
            send_sem=a_send.at[dz, dg], recv_sem=a_recv.at[dz, dg],
            device_id=(partner(g, dg), r, partner(c, dz)), device_id_type=MESH)
        copy.start()
        sends[dz, dg] = copy

    for dz in (2, 3, 1, 0):
        loads[dz].wait()
        for dg in range(4):
            if dz or dg:
                stage[dz, dg] = held[dz][sources[dg]]
            else:
                pieces[r, g, c] = held[0][sources[0]]
        if dz == 3:
            pl.semaphore_wait(barrier, 16)
            for dz_, dg in across_order:
                send(dz_, dg)
    for dz, dg in near_order:
        if dz or dg:
            send(dz, dg)
    load_omega = pltpu.make_async_copy(sketches, taken, om_sem)
    load_omega.start()
    load_omega.wait()
    omega = taken[sources[0]]

    forwards = {}

    def forward(dz, dg):
        spot = pieces.at[r, partner(g, dg), partner(c, dz)]
        copy = pltpu.make_async_remote_copy(
            src_ref=spot, dst_ref=spot, send_sem=f_send.at[dz, dg], recv_sem=f_recv.at[dz, dg],
            device_id=other, device_id_type=MESH)
        copy.start()
        forwards[dz, dg] = copy

    def pair_rows(side, dg, far):
        half = lax.rem(c // 2 + far, 2)
        start = ((side * 4 + partner(g, dg)) * 4 + 2 * half) * height
        return half, pl.ds(pl.multiple_of(start, 16), 2 * height)

    def settle(side, dg, far):
        half, place = pair_rows(side, dg, far)
        block[place, :] = pieces[side, partner(g, dg), pl.ds(2 * half, 2)].reshape(2 * height, wide)
        return half, place

    def sketch(dg, far):
        half, place = settle(r, dg, far)
        done = jnp.dot(block[place, :], omega, preferred_element_type=F32)
        into = pl.ds(pl.multiple_of(2 * height * half, 16), 2 * height)
        part1[partner(g, dg), into, :] = done.astype(BF16)

    pairs = [(dg, 0) for dg in (3, 1, 2, 0)] + [(dg, 1) for dg in range(4)]
    for i, (dg, far) in enumerate(pairs):
        for dz in ((0, 1), (2, 3))[far]:
            if dz or dg:
                sends[dz, dg].wait_recv()
            forward(dz, dg)
        if i:
            before = pairs[i - 1]
            for dz in ((0, 1), (2, 3))[before[1]]:
                forwards[dz, before[0]].wait_recv()
            settle(1 - r, *before)
        sketch(dg, far)

    def scatter(part, rs, send_sem, recv_sem, prepare_share=None):
        copies = []
        for dz in HOPS:
            k = partner(c, dz)
            if prepare_share:
                prepare_share(k)
            copy = pltpu.make_async_remote_copy(
                src_ref=part.at[k], dst_ref=rs.at[dz], send_sem=send_sem.at[dz],
                recv_sem=recv_sem.at[dz], device_id=(g, r, k), device_id_type=MESH)
            copy.start()
            copies.append(copy)
        if prepare_share:
            prepare_share(c)
        return copies

    def total(part, rs, copies):
        for copy in copies:
            copy.wait()
        found = part[c].astype(F32)
        for dz in HOPS:
            found = found + rs[dz].astype(F32)
        return found

    def gather(ref, g_send, g_recv, h_send, h_recv):
        def spot(k):
            return ref.at[pl.ds(pl.multiple_of(r * deep + k * share, 16), share), :]

        copies, passed = [], []

        def hand(dz):
            place = spot(partner(c, dz))
            copy = pltpu.make_async_remote_copy(
                src_ref=place, dst_ref=place, send_sem=h_send.at[dz], recv_sem=h_recv.at[dz],
                device_id=other, device_id_type=MESH)
            copy.start()
            passed.append(copy)

        for dz in HOPS:
            copy = pltpu.make_async_remote_copy(
                src_ref=spot(c), dst_ref=spot(c), send_sem=g_send.at[dz], recv_sem=g_recv.at[dz],
                device_id=(g, r, partner(c, dz)), device_id_type=MESH)
            copy.start()
            copies.append((dz, copy))
        hand(0)
        def finish():
            for dz, copy in sorted(copies, key=lambda pair: pair[0]):
                copy.wait_recv()
                hand(dz)
            for _, copy in copies:
                copy.wait_send()
            for copy in passed:
                copy.wait()
        return finish

    def own_rows(side):
        return pl.ds(pl.multiple_of(side * deep, 16), deep)

    copies = scatter(part1, rs1, s1_send, s1_recv)

    def kernel_block(side):
        found = lax.dot_general(block[own_rows(r), :], block[own_rows(side), :], NT,
                                preferred_element_type=F32)
        kernel_rows[side] = found.astype(BF16)

    kernel_block(r)
    sk[pl.ds(pl.multiple_of(r * deep + c * share, 16), share), :] = total(
        part1, rs1, copies).astype(BF16)
    finish = gather(sk, g1_send, g1_recv, h1_send, h1_recv)
    last = pairs[-1]
    for dz in (2, 3):
        forwards[dz, last[0]].wait_recv()
    settle(1 - r, *last)
    kernel_block(1 - r)
    finish()

    def power_share(k):
        place = pl.ds(pl.multiple_of(k * share, 16), share)
        found = (jnp.dot(kernel_rows[0, place, :], sk[:deep, :], preferred_element_type=F32)
                 + jnp.dot(kernel_rows[1, place, :], sk[deep:, :], preferred_element_type=F32))
        part2[k] = found.astype(BF16)

    mine = total(part2, rs2, scatter(part2, rs2, s2_send, s2_recv, power_share))
    power[pl.ds(pl.multiple_of(r * deep + c * share, 16), share), :] = mine.astype(BF16)
    own_power[...] = mine
    gather(power, g2_send, g2_recv, h2_send, h2_recv)()

    whole = power[...]
    tall[...] = whole.astype(F32).T.astype(BF16)
    gram = jnp.dot(tall[...], whole, preferred_element_type=F32)
    step = wide // 4

    def weigh(i):
        span = pl.ds(i * step, step)
        found = jnp.dot(tall[...], block[:, span], preferred_element_type=F32)
        high = found.astype(BF16)
        high_out[:, span] = high
        low_out[:, span] = (found - high.astype(F32)).astype(BF16)

    inverse = inverse_factor(gram, 32, weigh)
    factor_out[...] = inverse
    for copy in sends.values():
        copy.wait_send()
    for copy in forwards.values():
        copy.wait_send()


def project_kernel(cuts, own_power, factor, high, low, basis_out, projection,
                   shown, basis, basis_sem, out_sem):
    rank, wide = high.shape
    step = wide // cuts
    scaled = factor[...] * math.sqrt(4 * wide)
    above = scaled.astype(BF16)
    both = jnp.concatenate([above, (scaled - above.astype(F32)).astype(BF16)], axis=0)
    copies = []
    for i in range(cuts):
        span = pl.ds(i * step, step)
        found = jnp.dot(both, high[:, span], preferred_element_type=F32)
        small = jnp.dot(above, low[:, span], preferred_element_type=F32)
        shown[:, span] = found[:rank] + (found[rank:] + small)
        copy = pltpu.make_async_copy(shown.at[:, span], projection.at[0, :, span], out_sem.at[i])
        copy.start()
        copies.append(copy)
        if i == cuts // 2:
            basis[...] = lax.dot_general(
                own_power[...], factor[...], NT, precision=lax.Precision.HIGHEST,
                preferred_element_type=F32) * math.sqrt(8 * own_power.shape[0])
            last = pltpu.make_async_copy(basis, basis_out.at[0], basis_sem)
            last.start()
            copies.append(last)
    for copy in copies:
        copy.wait()


def fused_device(layer_windows, sketches, group_of):
    _, height, total_cols = layer_windows.shape
    rank = sketches.shape[2]
    wide = total_cols // 4
    rows = height * 32
    share = rows // 8
    cuts = 8
    vmem = pl.BlockSpec(memory_space=pltpu.VMEM)
    hbm = pl.BlockSpec(memory_space=pltpu.HBM)
    dma = pltpu.SemaphoreType.DMA
    own_power, factor, high, low = pl.pallas_call(
        range_kernel,
        out_shape=(
            jax.ShapeDtypeStruct((share, rank), F32),
            jax.ShapeDtypeStruct((rank, rank), F32),
            jax.ShapeDtypeStruct((rank, wide), BF16),
            jax.ShapeDtypeStruct((rank, wide), BF16),
        ),
        in_specs=[pl.BlockSpec(memory_space=pltpu.SMEM), hbm, hbm],
        out_specs=(vmem,) * 4,
        scratch_shapes=[
            pltpu.VMEM((rank, rows), BF16),
            *[pltpu.VMEM((4, height, wide), BF16)] * 4,
            pltpu.VMEM((4, 4, height, wide), BF16),
            pltpu.VMEM(sketches.shape, BF16),
            pltpu.VMEM((2, 4, 4, height, wide), BF16),
            pltpu.VMEM((rows, wide), BF16),
            pltpu.VMEM((2, rows // 2, rows // 2), BF16),
            pltpu.VMEM((4, share, rank), BF16),
            pltpu.VMEM((4, share, rank), BF16),
            pltpu.VMEM((4, share, rank), BF16),
            pltpu.VMEM((4, share, rank), BF16),
            pltpu.VMEM((rows, rank), BF16),
            pltpu.VMEM((rows, rank), BF16),
            dma((4,)), dma,
            dma((4, 4)), dma((4, 4)), dma((4, 4)), dma((4, 4)),
            dma((4,)), dma((4,)), dma((4,)), dma((4,)), dma((4,)), dma((4,)),
            dma((4,)), dma((4,)), dma((4,)), dma((4,)), dma((4,)), dma((4,)),
        ],
        compiler_params=pltpu.CompilerParams(
            collective_id=0, has_side_effects=True, vmem_limit_bytes=50 << 20),
        name="range_finder",
    )(group_of, layer_windows, sketches)
    return pl.pallas_call(
        functools.partial(project_kernel, cuts),
        out_shape=(
            jax.ShapeDtypeStruct((1, share, rank), F32),
            jax.ShapeDtypeStruct((1, rank, wide), F32),
        ),
        in_specs=[vmem] * 4,
        out_specs=(hbm, hbm),
        scratch_shapes=[pltpu.VMEM((rank, wide), F32), pltpu.VMEM((share, rank), F32), dma, dma((cuts,))],
        compiler_params=pltpu.CompilerParams(vmem_limit_bytes=8 << 20),
        name="project",
    )(own_power, factor, high, low)


def solution(mesh):
    in_specs = (P(None, ("row", "grp", "col"), None), P(None, "col", None), P())
    out_specs = (P("grp", ("row", "col"), None), P("grp", None, "col"))
    sizes = (mesh.shape["grp"], mesh.shape["row"], mesh.shape["col"])

    def body(layer_windows, sketches, group_of):
        count, height, total_cols = layer_windows.shape
        fits = sizes == (4, 2, 4) and count == 4 and height % 8 == 0 and height <= 32
        if fits and sketches.shape[2] == 128 and total_cols in (8192, 16384):
            return fused_device(layer_windows, sketches, group_of)
        return per_device(layer_windows, sketches, group_of)

    return jax.shard_map(body, mesh=mesh, in_specs=in_specs, out_specs=out_specs, check_vma=False)
```

```python
import functools
import math

import jax
import jax.numpy as jnp
from jax import lax
from jax.experimental import pallas as pl
from jax.experimental.pallas import tpu as pltpu
from jax.sharding import PartitionSpec as P

MESH = pl.DeviceIdType.MESH
F32 = jnp.float32
BF16 = jnp.bfloat16


def across(left, right):
    return lax.dot_general(
        left, right, (((0,), (0,)), ((), ())), preferred_element_type=jnp.float32
    )


def right_solve(lower, power):
    return lax.linalg.triangular_solve(lower, power, left_side=False, lower=True, transpose_a=True)


def owners(group_of):
    count = group_of.shape[0]
    slots = jnp.arange(count, dtype=jnp.int32)
    matched = (group_of[None, :] == slots[:, None]).astype(jnp.int32)
    return jnp.sum(matched * slots[None, :], axis=1)


def per_device(layer_windows, sketches, group_of):
    owner_of = owners(group_of)
    ordered = jnp.stack([
        lax.dynamic_index_in_dim(layer_windows, owner_of[j], 0, keepdims=False)
        for j in range(layer_windows.shape[0])
    ])
    block = lax.all_to_all(
        lax.all_to_all(ordered, "col", split_axis=2, concat_axis=1, tiled=True),
        "grp",
        split_axis=0,
        concat_axis=1,
        tiled=True,
    )[0]
    mine = owner_of[lax.axis_index("grp")]
    omega = lax.dynamic_index_in_dim(sketches, mine, 0, keepdims=False)
    total_rows = block.shape[0] * lax.axis_size("row")
    total_cols = block.shape[1] * lax.axis_size("col")
    share = block.shape[0] // lax.axis_size("col")

    def summed_rows(right):
        return lax.psum(jnp.dot(block, right, preferred_element_type=jnp.float32), "col")

    sketched = summed_rows(omega).astype(jnp.bfloat16)
    back = lax.psum(across(block, sketched).astype(jnp.bfloat16), "row")
    power = summed_rows(back)
    gram = lax.psum(
        jnp.dot(power.T, power, precision=lax.Precision.HIGHEST).astype(jnp.bfloat16), "row"
    ).astype(jnp.float32)
    lower = jnp.linalg.cholesky(gram)
    ortho = right_solve(lower, power) * math.sqrt(total_rows)
    basis_share = lax.dynamic_slice_in_dim(ortho, lax.axis_index("col") * share, share, 0)
    ortho_low = ortho.astype(jnp.bfloat16)
    projected = lax.psum(across(ortho_low, block).astype(jnp.bfloat16), "row").astype(
        jnp.float32
    ) * math.sqrt(total_cols / total_rows)
    return (basis_share[None], projected[None])


def thirds(array):
    high = array.astype(BF16)
    rest = array - high.astype(F32)
    middle = rest.astype(BF16)
    return high, middle, (rest - middle.astype(F32)).astype(BF16)


def across_rows(left, right):
    a, b, c = thirds(left)
    d, e, f = thirds(right)
    return lax.dot_general(
        jnp.concatenate([a, a, b, a, b, c], axis=0), jnp.concatenate([d, e, d, f, e, d], axis=0),
        (((0,), (0,)), ((), ())), preferred_element_type=F32)


def inverse_factor(gram, size, between):
    rank = gram.shape[0]
    tiles = size // 8
    line = lax.broadcasted_iota(jnp.int32, (8, rank), 0)
    down = lax.broadcasted_iota(jnp.int32, (rank, rank), 0)
    eye = (down == lax.broadcasted_iota(jnp.int32, (rank, rank), 1)).astype(F32)
    rest = jnp.concatenate([gram, eye], axis=1)
    done = []
    for p in range(0, rank, size):
        top, rest = rest[:size], rest[size:]
        panel = [top[8 * t:8 * t + 8] for t in range(tiles)]
        cols = [[jnp.broadcast_to(panel[t][:, p + k:p + k + 1], (8, rank)) if t >= k // 8 else None
                 for t in range(tiles)] for k in range(size)]
        pivots = [jnp.zeros((8, rank), F32) for _ in range(tiles)]
        for k in range(size):
            at, row = k // 8, k % 8
            pivot = cols[k][at][row:row + 1, :]
            pivots[at] = jnp.where(line == row, pivot, pivots[at])
            if k == size - 1:
                break
            over = 1.0 / pivot
            head = panel[at][row:row + 1, :]
            for t in range(at, tiles):
                factor = cols[k][t] * over
                if t == at:
                    factor = jnp.where(line > row, factor, 0.0)
                for l in range(k + 1, 8 * t + 8):
                    cols[l][t] = cols[l][t] - factor * cols[k][l // 8][l % 8:l % 8 + 1, :]
                panel[t] = panel[t] - jnp.concatenate([factor, factor], axis=1) * head
        scaled = jnp.concatenate(pivots, axis=0)
        full = jnp.concatenate(panel, axis=0)
        done.append(full[:, rank:] * lax.rsqrt(scaled))
        between(p // size)
        if p + size < rank:
            weights = full[:, :rank] * (1.0 / scaled)
            rest = rest - across_rows(weights[:, p + size:], full)
    return jnp.concatenate(done, axis=0)


def partner(index, step):
    return (index, index + 1 - 2 * lax.rem(index, 2), lax.rem(index + 2, 4), 3 - index)[step]


HOPS = (2, 3, 1)
NT = (((1,), (1,)), ((), ()))


def range_kernel(group_of, windows, sketches, own_power, factor_out, high_out, low_out, tall,
                 held0, held1, held2, held3, stage, taken, pieces, block, kernel_rows, part1, part2, rs1, rs2, sk, power,
                 in_sem, om_sem, a_send, a_recv, f_send, f_recv,
                 s1_send, s1_recv, g1_send, g1_recv, h1_send, h1_recv,
                 s2_send, s2_recv, g2_send, g2_recv, h2_send, h2_recv):
    g, r, c = lax.axis_index("grp"), lax.axis_index("row"), lax.axis_index("col")
    height = windows.shape[1]
    rows, wide = block.shape
    deep, share = rows // 2, rows // 8
    other = (g, 1 - r, c)

    def columns(z):
        return pl.ds(pl.multiple_of(z * wide, 128), wide)

    held = (held0, held1, held2, held3)
    loads = {}
    for dz in (2, 3, 1, 0):
        loads[dz] = pltpu.make_async_copy(
            windows.at[:, :, columns(partner(c, dz))], held[dz], in_sem.at[dz])
        loads[dz].start()
    barrier = pltpu.get_barrier_semaphore()
    for dz in range(4):
        for dg in range(4):
            if dz or dg:
                pl.semaphore_signal(barrier, inc=1, device_id=(partner(g, dg), r, partner(c, dz)),
                                    device_id_type=MESH)
    pl.semaphore_signal(barrier, inc=1, device_id=other, device_id_type=MESH)

    def owner(slot):
        found = jnp.int32(0)
        for m in range(4):
            found = jnp.where(group_of[m] == slot, jnp.int32(m), found)
        return found

    sources = [owner(partner(g, dg)) for dg in range(4)]
    across_order = [(dz, dg) for dg in range(4) for dz in (2, 3)]
    near_order = [(dz, dg) for dz in (1, 0) for dg in (3, 1, 2, 0)]

    sends = {}

    def send(dz, dg):
        copy = pltpu.make_async_remote_copy(
            src_ref=stage.at[dz, dg], dst_ref=pieces.at[r, g, c],
            send_sem=a_send.at[dz, dg], recv_sem=a_recv.at[dz, dg],
            device_id=(partner(g, dg), r, partner(c, dz)), device_id_type=MESH)
        copy.start()
        sends[dz, dg] = copy

    for dz in (2, 3, 1, 0):
        loads[dz].wait()
        for dg in range(4):
            if dz or dg:
                stage[dz, dg] = held[dz][sources[dg]]
            else:
                pieces[r, g, c] = held[0][sources[0]]
        if dz == 3:
            pl.semaphore_wait(barrier, 16)
            for dz_, dg in across_order:
                send(dz_, dg)
    for dz, dg in near_order:
        if dz or dg:
            send(dz, dg)
    load_omega = pltpu.make_async_copy(sketches, taken, om_sem)
    load_omega.start()
    load_omega.wait()
    omega = taken[sources[0]]

    forwards = {}

    def forward(dz, dg):
        spot = pieces.at[r, partner(g, dg), partner(c, dz)]
        copy = pltpu.make_async_remote_copy(
            src_ref=spot, dst_ref=spot, send_sem=f_send.at[dz, dg], recv_sem=f_recv.at[dz, dg],
            device_id=other, device_id_type=MESH)
        copy.start()
        forwards[dz, dg] = copy

    def pair_rows(side, dg, far):
        half = lax.rem(c // 2 + far, 2)
        start = ((side * 4 + partner(g, dg)) * 4 + 2 * half) * height
        return half, pl.ds(pl.multiple_of(start, 16), 2 * height)

    def settle(side, dg, far):
        half, place = pair_rows(side, dg, far)
        block[place, :] = pieces[side, partner(g, dg), pl.ds(2 * half, 2)].reshape(2 * height, wide)
        return half, place

    def sketch(dg, far):
        half, place = settle(r, dg, far)
        done = jnp.dot(block[place, :], omega, preferred_element_type=F32)
        into = pl.ds(pl.multiple_of(2 * height * half, 16), 2 * height)
        part1[partner(g, dg), into, :] = done.astype(BF16)

    pairs = [(dg, 0) for dg in (3, 1, 2, 0)] + [(dg, 1) for dg in range(4)]
    for i, (dg, far) in enumerate(pairs):
        for dz in ((0, 1), (2, 3))[far]:
            if dz or dg:
                sends[dz, dg].wait_recv()
            forward(dz, dg)
        if i:
            before = pairs[i - 1]
            for dz in ((0, 1), (2, 3))[before[1]]:
                forwards[dz, before[0]].wait_recv()
            settle(1 - r, *before)
        sketch(dg, far)

    left_over = []

    def scatter(part, rs, send_sem, recv_sem, prepare_share=None):
        copies = []
        for dz in HOPS:
            k = partner(c, dz)
            if prepare_share:
                prepare_share(k)
            copy = pltpu.make_async_remote_copy(
                src_ref=part.at[k], dst_ref=rs.at[dz], send_sem=send_sem.at[dz],
                recv_sem=recv_sem.at[dz], device_id=(g, r, k), device_id_type=MESH)
            copy.start()
            copies.append(copy)
        if prepare_share:
            prepare_share(c)
        return copies

    def total(part, rs, copies):
        for copy in copies:
            copy.wait_recv()
            left_over.append(copy)
        found = part[c].astype(F32)
        for dz in HOPS:
            found = found + rs[dz].astype(F32)
        return found

    def gather(ref, g_send, g_recv, h_send, h_recv):
        def spot(k):
            return ref.at[pl.ds(pl.multiple_of(r * deep + k * share, 16), share), :]

        copies, passed = [], []

        def hand(dz):
            place = spot(partner(c, dz))
            copy = pltpu.make_async_remote_copy(
                src_ref=place, dst_ref=place, send_sem=h_send.at[dz], recv_sem=h_recv.at[dz],
                device_id=other, device_id_type=MESH)
            copy.start()
            passed.append(copy)

        for dz in HOPS:
            copy = pltpu.make_async_remote_copy(
                src_ref=spot(c), dst_ref=spot(c), send_sem=g_send.at[dz], recv_sem=g_recv.at[dz],
                device_id=(g, r, partner(c, dz)), device_id_type=MESH)
            copy.start()
            copies.append((dz, copy))
        hand(0)
        def finish():
            for dz, copy in sorted(copies, key=lambda pair: pair[0]):
                copy.wait_recv()
                hand(dz)
            left_over.extend(copy for _, copy in copies)
            for copy in passed:
                copy.wait_recv()
                left_over.append(copy)
        return finish

    def own_rows(side):
        return pl.ds(pl.multiple_of(side * deep, 16), deep)

    copies = scatter(part1, rs1, s1_send, s1_recv)

    def kernel_block(side):
        found = lax.dot_general(block[own_rows(r), :], block[own_rows(side), :], NT,
                                preferred_element_type=F32)
        kernel_rows[side] = found.astype(BF16)

    kernel_block(r)
    sk[pl.ds(pl.multiple_of(r * deep + c * share, 16), share), :] = total(
        part1, rs1, copies).astype(BF16)
    finish = gather(sk, g1_send, g1_recv, h1_send, h1_recv)
    last = pairs[-1]
    for dz in (2, 3):
        forwards[dz, last[0]].wait_recv()
    settle(1 - r, *last)
    kernel_block(1 - r)
    finish()

    def power_share(k):
        place = pl.ds(pl.multiple_of(k * share, 16), share)
        found = (jnp.dot(kernel_rows[0, place, :], sk[:deep, :], preferred_element_type=F32)
                 + jnp.dot(kernel_rows[1, place, :], sk[deep:, :], preferred_element_type=F32))
        part2[k] = found.astype(BF16)

    mine = total(part2, rs2, scatter(part2, rs2, s2_send, s2_recv, power_share))
    power[pl.ds(pl.multiple_of(r * deep + c * share, 16), share), :] = mine.astype(BF16)
    own_power[...] = mine
    gather(power, g2_send, g2_recv, h2_send, h2_recv)()

    whole = power[...]
    tall[...] = whole.astype(F32).T.astype(BF16)
    gram = jnp.dot(tall[...], whole, preferred_element_type=F32)
    step = wide // 4

    def weigh(i):
        span = pl.ds(i * step, step)
        found = jnp.dot(tall[...], block[:, span], preferred_element_type=F32)
        high = found.astype(BF16)
        high_out[:, span] = high
        low_out[:, span] = (found - high.astype(F32)).astype(BF16)

    inverse = inverse_factor(gram, 32, weigh)
    factor_out[...] = inverse
    for copy in [*sends.values(), *left_over]:
        copy.wait_send()
    for copy in forwards.values():
        copy.wait_send()


def project_kernel(cuts, own_power, factor, high, low, basis_out, projection,
                   shown, basis, basis_sem, out_sem):
    rank, wide = high.shape
    step = wide // cuts
    scaled = factor[...] * math.sqrt(4 * wide)
    above = scaled.astype(BF16)
    both = jnp.concatenate([above, (scaled - above.astype(F32)).astype(BF16)], axis=0)
    copies = []
    for i in range(cuts):
        span = pl.ds(i * step, step)
        found = jnp.dot(both, high[:, span], preferred_element_type=F32)
        small = jnp.dot(above, low[:, span], preferred_element_type=F32)
        shown[:, span] = found[:rank] + (found[rank:] + small)
        copy = pltpu.make_async_copy(shown.at[:, span], projection.at[0, :, span], out_sem.at[i])
        copy.start()
        copies.append(copy)
        if i == cuts // 2:
            basis[...] = lax.dot_general(
                own_power[...], factor[...], NT, precision=lax.Precision.HIGHEST,
                preferred_element_type=F32) * math.sqrt(8 * own_power.shape[0])
            last = pltpu.make_async_copy(basis, basis_out.at[0], basis_sem)
            last.start()
            copies.append(last)
    for copy in copies:
        copy.wait()


def fused_device(layer_windows, sketches, group_of):
    _, height, total_cols = layer_windows.shape
    rank = sketches.shape[2]
    wide = total_cols // 4
    rows = height * 32
    share = rows // 8
    cuts = 8
    vmem = pl.BlockSpec(memory_space=pltpu.VMEM)
    hbm = pl.BlockSpec(memory_space=pltpu.HBM)
    dma = pltpu.SemaphoreType.DMA
    own_power, factor, high, low = pl.pallas_call(
        range_kernel,
        out_shape=(
            jax.ShapeDtypeStruct((share, rank), F32),
            jax.ShapeDtypeStruct((rank, rank), F32),
            jax.ShapeDtypeStruct((rank, wide), BF16),
            jax.ShapeDtypeStruct((rank, wide), BF16),
        ),
        in_specs=[pl.BlockSpec(memory_space=pltpu.SMEM), hbm, hbm],
        out_specs=(vmem,) * 4,
        scratch_shapes=[
            pltpu.VMEM((rank, rows), BF16),
            *[pltpu.VMEM((4, height, wide), BF16)] * 4,
            pltpu.VMEM((4, 4, height, wide), BF16),
            pltpu.VMEM(sketches.shape, BF16),
            pltpu.VMEM((2, 4, 4, height, wide), BF16),
            pltpu.VMEM((rows, wide), BF16),
            pltpu.VMEM((2, rows // 2, rows // 2), BF16),
            pltpu.VMEM((4, share, rank), BF16),
            pltpu.VMEM((4, share, rank), BF16),
            pltpu.VMEM((4, share, rank), BF16),
            pltpu.VMEM((4, share, rank), BF16),
            pltpu.VMEM((rows, rank), BF16),
            pltpu.VMEM((rows, rank), BF16),
            dma((4,)), dma,
            dma((4, 4)), dma((4, 4)), dma((4, 4)), dma((4, 4)),
            dma((4,)), dma((4,)), dma((4,)), dma((4,)), dma((4,)), dma((4,)),
            dma((4,)), dma((4,)), dma((4,)), dma((4,)), dma((4,)), dma((4,)),
        ],
        compiler_params=pltpu.CompilerParams(
            collective_id=0, has_side_effects=True, vmem_limit_bytes=50 << 20),
        name="range_finder",
    )(group_of, layer_windows, sketches)
    return pl.pallas_call(
        functools.partial(project_kernel, cuts),
        out_shape=(
            jax.ShapeDtypeStruct((1, share, rank), F32),
            jax.ShapeDtypeStruct((1, rank, wide), F32),
        ),
        in_specs=[vmem] * 4,
        out_specs=(hbm, hbm),
        scratch_shapes=[pltpu.VMEM((rank, wide), F32), pltpu.VMEM((share, rank), F32), dma, dma((cuts,))],
        compiler_params=pltpu.CompilerParams(vmem_limit_bytes=8 << 20),
        name="project",
    )(own_power, factor, high, low)


def solution(mesh):
    in_specs = (P(None, ("row", "grp", "col"), None), P(None, "col", None), P())
    out_specs = (P("grp", ("row", "col"), None), P("grp", None, "col"))
    sizes = (mesh.shape["grp"], mesh.shape["row"], mesh.shape["col"])

    def body(layer_windows, sketches, group_of):
        count, height, total_cols = layer_windows.shape
        fits = sizes == (4, 2, 4) and count == 4 and height % 8 == 0 and height <= 32
        if fits and sketches.shape[2] == 128 and total_cols in (8192, 16384):
            return fused_device(layer_windows, sketches, group_of)
        return per_device(layer_windows, sketches, group_of)

    return jax.shard_map(body, mesh=mesh, in_specs=in_specs, out_specs=out_specs, check_vma=False)
```
